128 devices in a mesh: group: 8 (over y_hi, x), fsdp: 16 (over z, y_lo, core).
Axes of the slice: x: 4, y: 4 (y_hi: 2, y_lo: 2; y = y_hi * 2 + y_lo), z: 4, core: 2. Of those that a mesh axis runs over, the one named last changes fastest.
Arguments:
- tokens_in: bfloat16 [131072, 2048], P(('group', 'fsdp')), may hold values from -6 to 6
- out_grad: bfloat16 [131072, 2048], P(('group', 'fsdp')), may hold values from -0.59765625 to 0.59765625
- w_in: bfloat16 [8, 2048, 8192], P('group', None, 'fsdp'), may hold values from -0.125 to 0.125
- w_out: bfloat16 [8, 8192, 2048], P('group', 'fsdp'), may hold values from -0.0625 to 0.0625
- chosen: int32 [128, 8, 16], P(('group', 'fsdp')), may hold values from 0 to 1023, as said below
- counts: int32 [128, 8], P(('group', 'fsdp')), may hold values from 1 to 16, as said below
- gates: float32 [128, 8, 16], P(('group', 'fsdp')), may hold values from 0.05 to 1
Outputs:
- grad_in: bfloat16 [131072, 2048], P(('group', 'fsdp'))
- grad_w_in: float32 [8, 2048, 8192], P('group', None, 'fsdp')
- grad_w_out: float32 [8, 8192, 2048], P('group', 'fsdp')
The draws below stay inside these ranges and needn't reach their ends.
Inputs may be any that keep to these rules, and one draw needn't show every extreme that they name: `chosen`: the 16 slots of one image and one expert name distinct positions. `counts`: each image fills all 16 slots of at least one expert.
All inputs are finite; a program needn't handle non-finite values.
Results may differ from the reference program's by a relative error of at most 0.0057.
Values may be sent and summed in bfloat16 or wider, within the bound.
A program may use at most 128 MiB of HBM per device.

```python
import math
import jax
import jax.numpy as jnp
from jax import lax

D = 2048
FF = 8192
LEN = 1024
CAP = 16
E_WIN = 8
IMAGES = 128
TOKENS = 131072


def draw_counts(key, part):
    count_key, pick_key = jax.random.split(jax.random.fold_in(key, 11))
    base_count = jax.random.randint(count_key, (IMAGES, E_WIN), max(1, CAP // 4), CAP + 1)
    full_expert = jax.random.randint(pick_key, (IMAGES, 1), 0, E_WIN)
    columns = lax.broadcasted_iota(jnp.int32, (IMAGES, E_WIN), 1)
    return jnp.where(columns == full_expert, CAP, base_count).astype(jnp.int32)


def draw_chosen(key, part):
    score_key = jax.random.fold_in(key, 23)
    scores = jax.random.randint(score_key, (IMAGES, E_WIN, LEN), 0, 2 ** 30 // LEN) * LEN
    scores = scores + lax.broadcasted_iota(jnp.int32, (IMAGES, E_WIN, LEN), 2)
    return lax.top_k(scores, CAP)[1].astype(jnp.int32)


def level_of(key, dims, shards, low, top_value):
    def one(dim, shards_of):
        draws = jax.random.uniform(jax.random.fold_in(jax.random.fold_in(key, 6), dim), (shards_of,), jnp.float32, low / len(shards), top_value / len(shards))
        return jnp.repeat(jnp.exp(draws), dims[dim] // shards_of).reshape((-1,) + (1,) * (len(dims) - dim - 1))

    level = one(*shards[0])
    for cut in shards[1:]:
        level = level * one(*cut)
    return level


def bell_draw(stream_key, extent, width, reach, shards=(), kind=jnp.bfloat16):
    values = width * jax.random.normal(stream_key, extent, jnp.float32)
    if shards:
        values = values * level_of(stream_key, extent, shards, -0.22, 0.18)
    return jnp.clip(values, -reach, reach).astype(kind)


def setup_inputs(seed: int = 0) -> dict:
    seeds = jax.random.split(jax.random.key(seed), 8)
    tokens_in = bell_draw(seeds[0], (TOKENS, D), 1.0, 6.0, ((0, 128),))
    out_grad = bell_draw(seeds[1], (TOKENS, D), 0.1, 0.59765625, ((0, 128),))
    w_in = bell_draw(seeds[2], (E_WIN, D, FF), D ** -0.5, 0.125, ((0, 8), (2, 16)))
    w_out = bell_draw(seeds[3], (E_WIN, FF, D), FF ** -0.5, 0.0625, ((0, 8), (1, 16)))
    chosen = draw_chosen(jax.random.fold_in(seeds[7], 71), 0)
    counts = draw_counts(jax.random.fold_in(seeds[7], 71), 0)
    gates = jnp.clip(jnp.exp(math.log(1.0) - 2.9957323 * jax.random.uniform(seeds[6], (IMAGES, E_WIN, CAP), jnp.float32) ** level_of(seeds[6], (IMAGES, E_WIN, CAP), ((0, 128),), -0.2, 0.2)), 0.05, 1.0)
    return dict(tokens_in=tokens_in, out_grad=out_grad, w_in=w_in, w_out=w_out, chosen=chosen, counts=counts, gates=gates)


gelu_coef = 0.7978845608028654


def gelu_parts(hidden):
    inner_arg = gelu_coef * (hidden + 0.044715 * hidden * hidden * hidden)
    tangent = jnp.tanh(inner_arg)
    activation = 0.5 * hidden * (1.0 + tangent)
    slope = 0.5 * (1.0 + tangent) + 0.5 * hidden * (1.0 - tangent * tangent) * gelu_coef * (1.0 + 3.0 * 0.044715 * hidden * hidden)
    return activation, slope


def reference(tokens_in, out_grad, w_in, w_out, chosen, counts, gates):
    image_base = (jnp.arange(IMAGES, dtype=jnp.int32) * LEN)[:, None, None]
    token_rows = (image_base + chosen).astype(jnp.int32)
    slot_iota = jnp.arange(CAP, dtype=jnp.int32)[None, None, :]
    live_gate = jnp.where(slot_iota < counts[:, :, None], gates, jnp.float32(0.0)).astype(jnp.float32)
    rows_by_expert = jnp.transpose(token_rows, (1, 0, 2)).reshape(E_WIN, IMAGES * CAP)
    gate_by_expert = jnp.transpose(live_gate, (1, 0, 2)).reshape(E_WIN, IMAGES * CAP)

    def per_expert(inputs):
        row_ids, gate_col, weight_in, weight_out = inputs
        expert_x = jnp.take(tokens_in, row_ids, axis=0)
        expert_grad = (gate_col[:, None] * jnp.take(out_grad, row_ids, axis=0).astype(jnp.float32)).astype(jnp.bfloat16)
        hidden = jnp.dot(expert_x, weight_in, preferred_element_type=jnp.float32)
        activation, slope = gelu_parts(hidden)
        activation = activation.astype(jnp.bfloat16)
        back_hidden = jnp.dot(expert_grad, weight_out.T, preferred_element_type=jnp.float32)
        hidden_grad = (back_hidden * slope).astype(jnp.bfloat16)
        grad_out_w = jnp.dot(activation.T, expert_grad, preferred_element_type=jnp.float32)
        grad_in_w = jnp.dot(expert_x.T, hidden_grad, preferred_element_type=jnp.float32)
        slot_grad = jnp.dot(hidden_grad, weight_in.T, preferred_element_type=jnp.float32)
        return grad_in_w, grad_out_w, slot_grad

    grad_w_in, grad_w_out, slot_grad = lax.map(per_expert, (rows_by_expert, gate_by_expert, w_in, w_out))
    summed = jnp.zeros((TOKENS, D), jnp.float32).at[rows_by_expert.reshape(-1)].add(slot_grad.reshape(E_WIN * IMAGES * CAP, D))
    return summed.astype(jnp.bfloat16), grad_w_in, grad_w_out
```

```python
import functools

import jax
import jax.numpy as jnp
from jax import lax
from jax.experimental import pallas as pl
from jax.experimental.pallas import tpu as pltpu
from jax.sharding import PartitionSpec as P

MESH = pl.DeviceIdType.MESH
gelu_coef = 0.7978845608028654
BF = jnp.bfloat16
F32 = jnp.float32


def gelu_parts(hidden):
    inner_arg = gelu_coef * (hidden + 0.044715 * hidden * hidden * hidden)
    tangent = jnp.tanh(inner_arg)
    activation = 0.5 * hidden * (1.0 + tangent)
    slope = 0.5 * (1.0 + tangent) + 0.5 * hidden * (1.0 - tangent * tangent) * gelu_coef * (
        1.0 + 3.0 * 0.044715 * hidden * hidden
    )
    return (activation, slope)


def slot_column(table):
    experts, slots = table.shape
    spread = jnp.concatenate(
        [jnp.broadcast_to(table[e : e + 1, :], (slots, slots)) for e in range(experts)], axis=0
    )
    row = lax.broadcasted_iota(jnp.int32, spread.shape, 0)
    lane = lax.broadcasted_iota(jnp.int32, spread.shape, 1)
    picked = jnp.where(lax.rem(row, slots) == lane, spread, jnp.zeros_like(spread))
    return jnp.sum(picked, axis=1, keepdims=True)


def one_hot_rows(chosen, length):
    column = slot_column(chosen.astype(F32)).astype(jnp.int32)
    lanes = lax.broadcasted_iota(jnp.int32, (column.shape[0], length), 1)
    return jnp.where(lanes == column, jnp.float32(1.0), jnp.float32(0.0)).astype(BF)


def pick_kernel(chosen_ref, counts_ref, gates_ref, x_ref, g_ref, px_ref, pg_ref):
    chosen = chosen_ref[0]
    slot_iota = lax.broadcasted_iota(jnp.int32, chosen.shape, 1)
    experts = chosen.shape[0]
    lane = lax.broadcasted_iota(jnp.int32, (experts, experts), 1)
    row = lax.broadcasted_iota(jnp.int32, (experts, experts), 0)
    limit = jnp.sum(
        jnp.where(lane == row, jnp.broadcast_to(counts_ref[...].astype(F32), (experts, experts)), 0.0),
        axis=1,
        keepdims=True,
    )
    live = jnp.where(slot_iota.astype(F32) < limit, gates_ref[0], jnp.float32(0.0))
    gate = slot_column(live)
    hot = one_hot_rows(chosen, x_ref.shape[0])
    px_ref[...] = jnp.dot(hot, x_ref[...], preferred_element_type=F32).astype(BF)
    pg_ref[...] = (gate * jnp.dot(hot, g_ref[...], preferred_element_type=F32)).astype(BF)


def pick_rows(tokens_in, out_grad, chosen, counts, gates):
    length, width = tokens_in.shape
    rows = chosen.shape[1] * chosen.shape[2]
    tile = 512
    whole = lambda a: pl.BlockSpec(a.shape, lambda i: (0,) * a.ndim)
    return pl.pallas_call(
        pick_kernel,
        grid=(width // tile,),
        in_specs=[
            whole(chosen),
            whole(counts),
            whole(gates),
            pl.BlockSpec((length, tile), lambda i: (0, i)),
            pl.BlockSpec((length, tile), lambda i: (0, i)),
        ],
        out_specs=[pl.BlockSpec((rows, tile), lambda i: (0, i))] * 2,
        out_shape=[jax.ShapeDtypeStruct((rows, width), BF)] * 2,
        name="pick_rows",
    )(chosen, counts, gates, tokens_in, out_grad)


def spread_kernel(chosen_ref, ret_ref, out_ref):
    hot = one_hot_rows(chosen_ref[0], out_ref.shape[0])
    out_ref[...] = lax.dot_general(
        hot, ret_ref[...], (((0,), (0,)), ((), ())), preferred_element_type=F32
    ).astype(BF)


def spread_rows(chosen, ret, length):
    rows, width = ret.shape
    tile = 512
    return pl.pallas_call(
        spread_kernel,
        grid=(width // tile,),
        in_specs=[
            pl.BlockSpec(chosen.shape, lambda i: (0, 0, 0)),
            pl.BlockSpec((rows, tile), lambda i: (0, i)),
        ],
        out_specs=pl.BlockSpec((length, tile), lambda i: (0, i)),
        out_shape=jax.ShapeDtypeStruct((length, width), BF),
        name="spread_rows",
    )(chosen, ret)


OWN, YY, ZM, ZP, OO, OY, MY, PY = range(8)
PIECE_M, PIECE_P, PIECE_Y, PIECE_A, PIECE_B, PIECE_OY, PIECE_MY, PIECE_PY = range(8)
RS_Y1, RS_A, RS_B, RS_LM, RS_LP, RS_M, RS_P, RS_Y = range(8)


def layer_kernel(
    groups,
    px,
    pg,
    win_hbm,
    wout_hbm,
    ret_ref,
    dwin_hbm,
    dwout_hbm,
    xbuf,
    gbuf,
    win,
    wout,
    act_t,
    hg_t,
    slope_buf,
    sg,
    pair,
    rs_y1,
    rs_half,
    rs_leaf,
    rs_last,
    fin,
    back,
    tiles,
    a_send,
    a_recv,
    own_sem,
    w_sem,
    ag_send,
    ag_recv,
    core_send,
    core_recv,
    pr_send,
    pr_recv,
    rs_send,
    rs_recv,
    d_send,
    d_recv,
    t_sem,
):
    g = lax.axis_index("group")
    f = lax.axis_index("fsdp")
    z, l, c = f // 4, lax.rem(f // 2, 2), lax.rem(f, 2)
    up, down, far = lax.rem(z + 1, 4), lax.rem(z + 3, 4), lax.rem(z + 2, 4)
    unit_of = {
        OWN: z * 2 + l,
        YY: z * 2 + (1 - l),
        ZM: down * 2 + l,
        ZP: up * 2 + l,
        OO: far * 2 + l,
        OY: far * 2 + (1 - l),
        MY: down * 2 + (1 - l),
        PY: up * 2 + (1 - l),
    }
    to_up, to_down = up * 4 + l * 2 + c, down * 4 + l * 2 + c
    to_y = z * 4 + (1 - l) * 2 + c
    to_core = z * 4 + l * 2 + (1 - c)
    CH = 128
    HALF = CH // 2
    SL = CH // groups

    def mine(u, start=0, size=CH):
        return pl.ds(pl.multiple_of((unit_of[u] * 2 + c) * CH + start, 16), size)

    def other(u):
        return pl.ds(pl.multiple_of((unit_of[u] * 2 + (1 - c)) * CH, 16), CH)

    barrier = pltpu.get_barrier_semaphore()
    for k in range(1, groups):
        pl.semaphore_signal(barrier, inc=1, device_id=(lax.rem(g + k, groups), f), device_id_type=MESH)
    for d in (to_up, to_down, to_y, to_core):
        pl.semaphore_signal(barrier, inc=1, device_id=(g, d), device_id_type=MESH)
    w_copies = [
        pltpu.make_async_copy(win_hbm.at[0], win, w_sem.at[0]),
        pltpu.make_async_copy(wout_hbm.at[0], wout, w_sem.at[1]),
    ]
    for w in w_copies:
        w.start()
    pl.semaphore_wait(barrier, groups - 1 + 4)

    bufs = (xbuf, gbuf)
    picked = (px, pg)
    pending = []

    def a_copy(a, k):
        dest = lax.rem(g + k, groups)
        return pltpu.make_async_remote_copy(
            src_ref=picked[a].at[pl.ds(pl.multiple_of(dest * SL, 16), SL)],
            dst_ref=bufs[a].at[pl.ds(pl.multiple_of(f * CH + g * SL, 16), SL)],
            send_sem=a_send.at[a, k - 1],
            recv_sem=a_recv.at[a, k - 1],
            device_id=(dest, f),
            device_id_type=MESH,
        )

    def a_arrival(a, k):
        source = lax.rem(g + groups - k, groups)
        here = bufs[a].at[pl.ds(pl.multiple_of(f * CH + source * SL, 16), SL)]
        return pltpu.make_async_remote_copy(
            src_ref=here,
            dst_ref=here,
            send_sem=a_send.at[a, k - 1],
            recv_sem=a_recv.at[a, k - 1],
            device_id=(source, f),
            device_id_type=MESH,
        )

    own_copies = []
    for a in range(2):
        for k in range(1, groups):
            copy = a_copy(a, k)
            copy.start()
            pending.append(copy)
        own = pltpu.make_async_copy(
            picked[a].at[pl.ds(pl.multiple_of(g * SL, 16), SL)],
            bufs[a].at[pl.ds(pl.multiple_of(f * CH + g * SL, 16), SL)],
            own_sem.at[a],
        )
        own.start()
        own_copies.append(own)

    def ag(a, rows, dest, piece, send):
        copy = pltpu.make_async_remote_copy(
            src_ref=bufs[a].at[rows],
            dst_ref=bufs[a].at[rows],
            send_sem=ag_send.at[a, send],
            recv_sem=ag_recv.at[a, piece],
            device_id=(g, dest),
            device_id_type=MESH,
        )
        return copy

    def ag_start(a, rows, dest, piece):
        copy = ag(a, rows, dest, piece, piece)
        copy.start()
        pending.append(copy)

    def ag_wait(a, rows, piece):
        ag(a, rows, to_y, piece, piece).wait_recv()

    def core(a, rows, u):
        return pltpu.make_async_remote_copy(
            src_ref=bufs[a].at[rows],
            dst_ref=bufs[a].at[rows],
            send_sem=core_send.at[a, u],
            recv_sem=core_recv.at[a, u],
            device_id=(g, to_core),
            device_id_type=MESH,
        )

    def core_start(a, u):
        copy = core(a, mine(u), u)
        copy.start()
        pending.append(copy)

    def core_wait(a, u):
        core(a, other(u), u).wait_recv()

    def unit_rows(u):
        return pl.ds(pl.multiple_of(unit_of[u] * 2 * CH, 2 * CH), 2 * CH)

    def forward(u):
        core_wait(0, u)
        rows = unit_rows(u)
        hidden = jnp.dot(xbuf[rows, :], win[...], preferred_element_type=F32)
        activation, slope = gelu_parts(hidden)
        act_t[:, rows] = activation.T.astype(BF)
        slope_buf[rows, :] = slope

    def pair_copy(u, rows):
        return pltpu.make_async_remote_copy(
            src_ref=sg.at[rows],
            dst_ref=pair.at[unit_of[u]],
            send_sem=pr_send.at[u],
            recv_sem=pr_recv.at[u],
            device_id=(g, to_core),
            device_id_type=MESH,
        )

    def backward(u):
        core_wait(1, u)
        rows = unit_rows(u)
        back_hidden = lax.dot_general(
            gbuf[rows, :], wout[...], (((1,), (1,)), ((), ())), preferred_element_type=F32
        )
        hidden_grad = back_hidden * slope_buf[rows, :]
        hg_t[:, rows] = hidden_grad.T.astype(BF)
        hidden_grad = hidden_grad.astype(BF)

        @pl.loop(0, 4)
        def _(j):
            cols = pl.ds(pl.multiple_of(j * 512, 512), 512)
            part = lax.dot_general(
                hidden_grad, win[cols, :], (((1,), (1,)), ((), ())), preferred_element_type=F32
            )
            sg[rows, cols] = part.astype(BF)

        copy = pair_copy(u, other(u))
        copy.start()
        pending.append(copy)

    def accumulate(base, size, load):
        @pl.loop(0, size // 16)
        def _(i):
            rows = pl.ds(pl.multiple_of(base + i * 16, 16), 16)
            total = sg[rows, :].astype(F32)
            sg[rows, :] = (total + load(i)).astype(BF)

    def chunk_start(u):
        return (unit_of[u] * 2 + c) * CH

    def block(i):
        return pl.ds(pl.multiple_of(i * 16, 16), 16)

    def pair_add(u):
        pair_copy(u, mine(u)).wait_recv()
        slab = pair.at[unit_of[u]]
        accumulate(chunk_start(u), CH, lambda i: slab[block(i), :].astype(F32))

    def rs(rows, dst, idx, dest):
        return pltpu.make_async_remote_copy(
            src_ref=sg.at[rows],
            dst_ref=dst,
            send_sem=rs_send.at[idx],
            recv_sem=rs_recv.at[idx],
            device_id=(g, dest),
            device_id_type=MESH,
        )

    def rs_start(rows, dst, idx, dest):
        copy = rs(rows, dst, idx, dest)
        copy.start()
        pending.append(copy)

    def rs_wait(dst, idx, size=CH):
        rs(mine(OWN, 0, size), dst, idx, to_y).wait_recv()

    def tile_copies(slot, j):
        cols = pl.ds(pl.multiple_of(j * 256, 256), 256)
        return (
            pltpu.make_async_copy(tiles[0].at[slot], dwin_hbm.at[0, cols, :], t_sem.at[0, slot]),
            pltpu.make_async_copy(tiles[1].at[slot], dwout_hbm.at[0, :, cols], t_sem.at[1, slot]),
        )

    def weight_tiles(first, last):
        @pl.loop(first, last)
        def _(j):
            slot = lax.rem(j, 2)
            cols = pl.ds(pl.multiple_of(j * 256, 256), 256)
            into, outof = tile_copies(slot, j)

            @pl.when(j >= 2)
            def _():
                into.wait()
                outof.wait()

            tiles[0][slot] = jnp.dot(hg_t[...], xbuf[:, cols], preferred_element_type=F32).T
            into.start()
            tiles[1][slot] = jnp.dot(act_t[...], gbuf[:, cols], preferred_element_type=F32)
            outof.start()

    for a in range(2):
        own_copies[a].wait()
        for k in range(1, groups):
            a_arrival(a, k).wait_recv()
        ag_start(a, mine(OWN), to_up, PIECE_M)
        ag_start(a, mine(OWN), to_down, PIECE_P)
        ag_start(a, mine(OWN), to_y, PIECE_Y)
        core_start(a, OWN)
    for w in w_copies:
        w.wait()
    forward(OWN)
    backward(OWN)

    ag_wait(0, mine(ZM), PIECE_M)
    ag_start(0, mine(ZM, 0, HALF), to_up, PIECE_A)
    core_start(0, ZM)
    ag_wait(0, mine(ZP), PIECE_P)
    ag_start(0, mine(ZP, HALF, HALF), to_down, PIECE_B)
    core_start(0, ZP)
    ag_wait(0, mine(YY), PIECE_Y)
    core_start(0, YY)
    pair_add(OWN)
    forward(ZM)
    forward(ZP)
    forward(YY)
    ag_wait(1, mine(ZM), PIECE_M)
    ag_start(1, mine(ZM, 0, HALF), to_up, PIECE_A)
    core_start(1, ZM)
    ag_wait(1, mine(ZP), PIECE_P)
    ag_start(1, mine(ZP, HALF, HALF), to_down, PIECE_B)
    core_start(1, ZP)
    ag_start(0, mine(YY), to_up, PIECE_MY)
    ag_start(0, mine(YY), to_down, PIECE_PY)
    ag_wait(1, mine(YY), PIECE_Y)
    ag_start(1, mine(YY), to_up, PIECE_MY)
    ag_start(1, mine(YY), to_down, PIECE_PY)
    core_start(1, YY)
    backward(ZM)
    backward(ZP)
    pair_add(ZM)

    ag_wait(0, mine(OO, 0, HALF), PIECE_A)
    ag_wait(0, mine(OO, HALF, HALF), PIECE_B)
    ag_start(0, mine(OO), to_y, PIECE_OY)
    core_start(0, OO)
    backward(YY)
    pair_add(ZP)
    ag_wait(1, mine(OO, 0, HALF), PIECE_A)
    ag_wait(1, mine(OO, HALF, HALF), PIECE_B)
    ag_start(1, mine(OO), to_y, PIECE_OY)
    core_start(1, OO)
    forward(OO)
    pair_add(YY)
    backward(OO)

    ag_wait(0, mine(OY), PIECE_OY)
    core_start(0, OY)
    pair_add(OO)
    forward(OY)
    ag_wait(0, mine(MY), PIECE_MY)
    core_start(0, MY)
    ag_wait(0, mine(PY), PIECE_PY)
    core_start(0, PY)
    forward(MY)
    forward(PY)
    ag_wait(1, mine(OY), PIECE_OY)
    core_start(1, OY)
    backward(OY)
    ag_wait(1, mine(MY), PIECE_MY)
    core_start(1, MY)
    ag_wait(1, mine(PY), PIECE_PY)
    core_start(1, PY)
    pair_add(OY)
    rs_start(mine(OY), rs_y1, RS_Y1, to_y)
    backward(MY)
    backward(PY)

    pair_add(MY)
    rs_start(mine(MY), rs_leaf.at[1], RS_LP, to_down)
    pair_add(PY)
    rs_wait(rs_y1, RS_Y1)
    accumulate(chunk_start(OO), CH, lambda i: rs_y1[block(i), :].astype(F32))
    rs_start(mine(OO, 0, HALF), rs_half.at[0], RS_A, to_down)
    rs_start(mine(OO, HALF, HALF), rs_half.at[1], RS_B, to_up)
    rs_start(mine(PY), rs_leaf.at[0], RS_LM, to_up)
    weight_tiles(0, 2)
    rs_wait(rs_half.at[0], RS_A, HALF)
    accumulate(chunk_start(ZM), HALF, lambda i: rs_half[0, block(i), :].astype(F32))
    rs_start(mine(ZM), rs_last.at[1], RS_P, to_down)
    rs_wait(rs_half.at[1], RS_B, HALF)
    accumulate(chunk_start(ZP) + HALF, HALF, lambda i: rs_half[1, block(i), :].astype(F32))
    rs_start(mine(ZP), rs_last.at[0], RS_M, to_up)
    weight_tiles(2, 6)
    rs_wait(rs_leaf.at[0], RS_LM)
    rs_wait(rs_leaf.at[1], RS_LP)
    accumulate(
        chunk_start(YY),
        CH,
        lambda i: rs_leaf[0, block(i), :].astype(F32) + rs_leaf[1, block(i), :].astype(F32),
    )
    rs_start(mine(YY), rs_last.at[2], RS_Y, to_y)
    weight_tiles(6, 8)
    rs_wait(rs_last.at[0], RS_M)
    rs_wait(rs_last.at[1], RS_P)
    rs_wait(rs_last.at[2], RS_Y)

    @pl.loop(0, CH // 16)
    def _(i):
        rows = pl.ds(pl.multiple_of(chunk_start(OWN) + i * 16, 16), 16)
        total = sg[rows, :].astype(F32) + rs_last[0, block(i), :].astype(F32)
        total = total + rs_last[1, block(i), :].astype(F32) + rs_last[2, block(i), :].astype(F32)
        fin[block(i), :] = total.astype(BF)

    def d_copy(k):
        dest = lax.rem(g + k, groups)
        return pltpu.make_async_remote_copy(
            src_ref=fin.at[pl.ds(pl.multiple_of(dest * SL, 16), SL)],
            dst_ref=back.at[pl.ds(pl.multiple_of(g * SL, 16), SL)],
            send_sem=d_send.at[k - 1],
            recv_sem=d_recv.at[k - 1],
            device_id=(dest, f),
            device_id_type=MESH,
        )

    def d_arrival(k):
        source = lax.rem(g + groups - k, groups)
        return pltpu.make_async_remote_copy(
            src_ref=fin.at[pl.ds(0, SL)],
            dst_ref=back.at[pl.ds(pl.multiple_of(source * SL, 16), SL)],
            send_sem=d_send.at[k - 1],
            recv_sem=d_recv.at[k - 1],
            device_id=(source, f),
            device_id_type=MESH,
        )

    for k in range(1, groups):
        copy = d_copy(k)
        copy.start()
        pending.append(copy)
    own_rows = pl.ds(pl.multiple_of(g * SL, 16), SL)
    back[own_rows, :] = fin[own_rows, :]
    for slot in range(2):
        into, outof = tile_copies(slot, 6 + slot)
        into.wait()
        outof.wait()
    for k in range(1, groups):
        d_arrival(k).wait_recv()
    ret_ref[...] = back[...]
    for copy in pending:
        copy.wait_send()


def layer(px, pg, w_in, w_out):
    groups = lax.axis_size("group")
    rows, width = px.shape
    hidden = w_in.shape[2]
    total = rows * lax.axis_size("fsdp")
    vmem, dma = pltpu.VMEM, pltpu.SemaphoreType.DMA
    return pl.pallas_call(
        functools.partial(layer_kernel, groups),
        out_shape=[
            jax.ShapeDtypeStruct((rows, width), BF),
            jax.ShapeDtypeStruct((1, width, hidden), F32),
            jax.ShapeDtypeStruct((1, hidden, width), F32),
        ],
        in_specs=[pl.BlockSpec(memory_space=pltpu.VMEM)] * 2 + [pl.BlockSpec(memory_space=pl.ANY)] * 2,
        out_specs=[pl.BlockSpec(memory_space=pltpu.VMEM)] + [pl.BlockSpec(memory_space=pl.ANY)] * 2,
        scratch_shapes=[
            vmem((total, width), BF),
            vmem((total, width), BF),
            vmem((width, hidden), BF),
            vmem((hidden, width), BF),
            vmem((hidden, total), BF),
            vmem((hidden, total), BF),
            vmem((total, hidden), F32),
            vmem((total, width), BF),
            vmem((8, rows, width), BF),
            vmem((rows, width), BF),
            vmem((2, rows // 2, width), BF),
            vmem((2, rows, width), BF),
            vmem((3, rows, width), BF),
            vmem((rows, width), BF),
            vmem((rows, width), BF),
            [vmem((2, 256, hidden), F32), vmem((2, hidden, 256), F32)],
            dma((2, groups - 1)),
            dma((2, groups - 1)),
            dma((2,)),
            dma((2,)),
            dma((2, 8)),
            dma((2, 8)),
            dma((2, 8)),
            dma((2, 8)),
            dma((8,)),
            dma((8,)),
            dma((8,)),
            dma((8,)),
            dma((groups - 1,)),
            dma((groups - 1,)),
            dma((2, 2)),
        ],
        compiler_params=pltpu.CompilerParams(
            collective_id=0, has_side_effects=True, vmem_limit_bytes=62 * 1024 * 1024
        ),
        name="layer",
    )(px, pg, w_in, w_out)


def shards(tokens_in, out_grad, w_in, w_out, chosen, counts, gates):
    px, pg = pick_rows(tokens_in, out_grad, chosen, counts, gates)
    ret, grad_w_in, grad_w_out = layer(px, pg, w_in, w_out)
    grad_in = spread_rows(chosen, ret, tokens_in.shape[0])
    return (grad_in, grad_w_in, grad_w_out)


def solution(mesh):
    placed = (
        P(("group", "fsdp"), None),
        P(("group", "fsdp"), None),
        P("group", None, "fsdp"),
        P("group", "fsdp", None),
        P(("group", "fsdp"), None, None),
        P(("group", "fsdp"), None),
        P(("group", "fsdp"), None, None),
    )
    return jax.shard_map(
        shards,
        mesh=mesh,
        in_specs=placed,
        out_specs=(P(("group", "fsdp"), None), P("group", None, "fsdp"), P("group", "fsdp", None)),
        check_vma=False,
    )
```

```python
import jax
import jax.numpy as jnp
from jax import lax
from jax.experimental import pallas as pl
from jax.experimental.pallas import tpu as pltpu
from jax.sharding import PartitionSpec as P

MESH = pl.DeviceIdType.MESH
gelu_coef = 0.7978845608028654
BF = jnp.bfloat16
F32 = jnp.float32


def gelu_parts(hidden):
    inner_arg = gelu_coef * (hidden + 0.044715 * hidden * hidden * hidden)
    tangent = jnp.tanh(inner_arg)
    activation = 0.5 * hidden * (1.0 + tangent)
    slope = 0.5 * (1.0 + tangent) + 0.5 * hidden * (1.0 - tangent * tangent) * gelu_coef * (
        1.0 + 3.0 * 0.044715 * hidden * hidden
    )
    return (activation, slope)


def slot_column(table):
    experts, slots = table.shape
    spread = jnp.concatenate(
        [jnp.broadcast_to(table[e : e + 1, :], (slots, slots)) for e in range(experts)], axis=0
    )
    row = lax.broadcasted_iota(jnp.int32, spread.shape, 0)
    lane = lax.broadcasted_iota(jnp.int32, spread.shape, 1)
    picked = jnp.where(lax.rem(row, slots) == lane, spread, jnp.zeros_like(spread))
    return jnp.sum(picked, axis=1, keepdims=True)


def one_hot_rows(chosen, length):
    column = slot_column(chosen.astype(F32)).astype(jnp.int32)
    lanes = lax.broadcasted_iota(jnp.int32, (column.shape[0], length), 1)
    return jnp.where(lanes == column, jnp.float32(1.0), jnp.float32(0.0)).astype(BF)


def spread_kernel(chosen_ref, ret_ref, out_ref):
    tile = out_ref.shape[0]
    column = slot_column(chosen_ref[0].astype(F32)).astype(jnp.int32) - pl.program_id(0) * tile
    lanes = lax.broadcasted_iota(jnp.int32, (column.shape[0], tile), 1)
    hot = jnp.where(lanes == column, jnp.float32(1.0), jnp.float32(0.0)).astype(BF)
    out_ref[...] = lax.dot_general(
        hot, ret_ref[...], (((0,), (0,)), ((), ())), preferred_element_type=F32
    ).astype(BF)


def spread_rows(chosen, ret, length):
    rows, width = ret.shape
    tile = 256
    return pl.pallas_call(
        spread_kernel,
        grid=(length // tile,),
        in_specs=[
            pl.BlockSpec(chosen.shape, lambda i: (0, 0, 0)),
            pl.BlockSpec((rows, width), lambda i: (0, 0)),
        ],
        out_specs=pl.BlockSpec((tile, width), lambda i: (i, 0)),
        out_shape=jax.ShapeDtypeStruct((length, width), BF),
        name="spread_rows",
    )(chosen, ret)


OWN, YY, ZM, ZP, OO, OY, MY, PY = range(8)
PIECE_M, PIECE_P, PIECE_Y, PIECE_A, PIECE_B, PIECE_OY, PIECE_MY, PIECE_PY = range(8)
RS_Y1, RS_A, RS_B, RS_LM, RS_LP, RS_M0, RS_M1, RS_P0, RS_P1, RS_Y = range(10)
CH = 64
HALF = CH // 2
SL = 16


def layer_kernel(
    chosen_ref,
    counts_ref,
    gates_ref,
    tok_hbm,
    cot_hbm,
    win_hbm,
    wout_hbm,
    ret_ref,
    dwin_hbm,
    dwout_hbm,
    px,
    pg,
    hot,
    xbuf,
    gbuf,
    win,
    wout,
    act_t,
    hg_t,
    slope_buf,
    sg,
    pair,
    rs_y1,
    rs_half,
    rs_leaf,
    rs_last,
    fin,
    back,
    tile_in,
    tile_out,
    tok_sem,
    a_send,
    a_recv,
    own_sem,
    w_sem,
    ag_send,
    ag_recv,
    core_send,
    core_recv,
    pr_send,
    pr_recv,
    rs_send,
    rs_recv,
    d_send,
    d_recv,
    t_sem,
):
    g = lax.axis_index("group")
    f = lax.axis_index("fsdp")
    h, x = g // 4, lax.rem(g, 4)
    z, l, c = f // 4, lax.rem(f // 2, 2), lax.rem(f, 2)
    up, down, far = lax.rem(z + 1, 4), lax.rem(z + 3, 4), lax.rem(z + 2, 4)
    unit_of = {
        OWN: z * 2 + l,
        YY: z * 2 + (1 - l),
        ZM: down * 2 + l,
        ZP: up * 2 + l,
        OO: far * 2 + l,
        OY: far * 2 + (1 - l),
        MY: down * 2 + (1 - l),
        PY: up * 2 + (1 - l),
    }
    to_up, to_down = up * 4 + l * 2 + c, down * 4 + l * 2 + c
    to_y = z * 4 + (1 - l) * 2 + c
    to_core = z * 4 + l * 2 + (1 - c)
    batch_rows = 16 * CH

    hops = [(0, 1), (0, 2), (0, 3), (1, 0), (1, 1), (1, 2), (1, 3)]

    def partner(b, k):
        px_ = lax.rem(x + k, 4)
        return (h * 4 + px_, f) if b == 0 else ((1 - h) * 4 + px_, to_y)

    def source_x(k):
        return lax.rem(x + 4 - k, 4)

    def ds(start, size):
        return pl.ds(pl.multiple_of(start, 16), size)

    def chunk(b, u, which):
        return b * batch_rows + (unit_of[u] * 2 + which) * CH

    def mine(b, u, start=0, size=CH):
        return ds(chunk(b, u, c) + start, size)

    def other(b, u):
        return ds(chunk(b, u, 1 - c), CH)

    def unit_rows(b, u):
        return pl.ds(pl.multiple_of(b * batch_rows + unit_of[u] * 2 * CH, 2 * CH), 2 * CH)

    length = tok_hbm.shape[0]
    width = tok_hbm.shape[1]
    token_copies = []
    for a, source in enumerate((tok_hbm, cot_hbm)):
        for j in range(4):
            cols = pl.ds(j * (width // 4), width // 4)
            copy = pltpu.make_async_copy(
                source.at[:, cols], sg.at[pl.ds(a * length, length), cols], tok_sem.at[a, j]
            )
            copy.start()
            token_copies.append(copy)
    w_copies = [
        pltpu.make_async_copy(win_hbm.at[0], win, w_sem.at[0]),
        pltpu.make_async_copy(wout_hbm.at[0], wout, w_sem.at[1]),
    ]
    for w in w_copies:
        w.start()
    barrier = pltpu.get_barrier_semaphore()
    for b, k in hops:
        pl.semaphore_signal(barrier, inc=1, device_id=partner(b, k), device_id_type=MESH)
    for d in (to_up, to_down, to_y, to_core):
        pl.semaphore_signal(barrier, inc=1, device_id=(g, d), device_id_type=MESH)

    hot[...] = one_hot_rows(chosen_ref[0], length)
    slot_iota = lax.broadcasted_iota(jnp.int32, chosen_ref.shape[1:], 1)
    experts = chosen_ref.shape[1]
    lane = lax.broadcasted_iota(jnp.int32, (experts, experts), 1)
    row = lax.broadcasted_iota(jnp.int32, (experts, experts), 0)
    limit = jnp.sum(
        jnp.where(lane == row, jnp.broadcast_to(counts_ref[...].astype(F32), (experts, experts)), 0.0),
        axis=1,
        keepdims=True,
    )
    live = jnp.where(slot_iota.astype(F32) < limit, gates_ref[0], jnp.float32(0.0))
    gate = slot_column(live)

    bufs = (xbuf, gbuf)
    picked = (px, pg)
    pending = []

    def start(copy):
        copy.start()
        pending.append(copy)

    def remote(src, dst, send, recv, dest):
        return pltpu.make_async_remote_copy(
            src_ref=src, dst_ref=dst, send_sem=send, recv_sem=recv, device_id=dest, device_id_type=MESH
        )

    def a_start(a, i):
        b, k = hops[i]
        dest = partner(b, k)
        start(
            remote(
                picked[a].at[ds(dest[0] * SL, SL)],
                bufs[a].at[ds(b * batch_rows + dest[1] * CH + x * SL, SL)],
                a_send.at[a, i],
                a_recv.at[a, i],
                dest,
            )
        )

    def a_wait(a, batch):
        for i, (b, k) in enumerate(hops):
            if b == batch:
                here = bufs[a].at[ds(b * batch_rows + f * CH + source_x(k) * SL, SL)]
                remote(here, here, a_send.at[a, i], a_recv.at[a, i], (g, to_y)).wait_recv()

    own_copies = []
    for a in range(2):
        for j in range(4):
            cols = pl.ds(j * (width // 4), width // 4)
            token_copies[a * 4 + j].wait()
            rows = jnp.dot(hot[...], sg[pl.ds(a * length, length), cols], preferred_element_type=F32)
            picked[a][:, cols] = (rows if a == 0 else gate * rows).astype(BF)
        if a == 0:
            pl.semaphore_wait(barrier, len(hops) + 4)
        for i in range(3):
            a_start(a, i)
        own = pltpu.make_async_copy(
            picked[a].at[ds(g * SL, SL)], bufs[a].at[ds(f * CH + x * SL, SL)], own_sem.at[a]
        )
        own.start()
        own_copies.append(own)
        if a == 1:
            for aa in range(2):
                for i in range(3, 7):
                    a_start(aa, i)

    def ag(a, b, rows, dest, piece):
        return remote(
            bufs[a].at[rows], bufs[a].at[rows], ag_send.at[a, b, piece], ag_recv.at[a, b, piece], (g, dest)
        )

    def ag_wait(a, b, rows, piece):
        ag(a, b, rows, to_y, piece).wait_recv()

    def core(a, b, u, rows):
        return remote(
            bufs[a].at[rows], bufs[a].at[rows], core_send.at[a, b, u], core_recv.at[a, b, u], (g, to_core)
        )

    def core_start(a, b, u):
        start(core(a, b, u, mine(b, u)))

    def core_wait(a, b, u):
        core(a, b, u, other(b, u)).wait_recv()

    def rows_of(ref, b, us):
        return jnp.concatenate([ref[unit_rows(b, u), :] for u in us], axis=0)

    def forward(b, us):
        for u in us:
            core_wait(0, b, u)
        hidden = jnp.dot(rows_of(xbuf, b, us), win[...], preferred_element_type=F32)
        activation, slope = gelu_parts(hidden)
        turned = activation.T.astype(BF)
        for i, u in enumerate(us):
            part = slice(i * 2 * CH, (i + 1) * 2 * CH)
            act_t[:, unit_rows(b, u)] = turned[:, part]
            slope_buf[unit_rows(b, u), :] = slope[part, :]

    def pair_copy(b, u, rows):
        return remote(
            sg.at[rows], pair.at[b, unit_of[u]], pr_send.at[b, u], pr_recv.at[b, u], (g, to_core)
        )

    def backward(b, us):
        for u in us:
            core_wait(1, b, u)
        back_hidden = lax.dot_general(
            rows_of(gbuf, b, us), wout[...], (((1,), (1,)), ((), ())), preferred_element_type=F32
        )
        hidden_grad = back_hidden * rows_of(slope_buf, b, us)
        turned = hidden_grad.T.astype(BF)
        for i, u in enumerate(us):
            hg_t[:, unit_rows(b, u)] = turned[:, i * 2 * CH : (i + 1) * 2 * CH]
        hidden_grad = hidden_grad.astype(BF)

        @pl.loop(0, 4)
        def _(j):
            cols = pl.ds(pl.multiple_of(j * 512, 512), 512)
            part = lax.dot_general(
                hidden_grad, win[cols, :], (((1,), (1,)), ((), ())), preferred_element_type=F32
            ).astype(BF)
            for i, u in enumerate(us):
                sg[unit_rows(b, u), cols] = part[i * 2 * CH : (i + 1) * 2 * CH, :]

        for u in us:
            start(pair_copy(b, u, other(b, u)))

    def accumulate(base, size, load):
        @pl.loop(0, size // 16)
        def _(i):
            rows = ds(base + i * 16, 16)
            total = sg[rows, :].astype(F32)
            sg[rows, :] = (total + load(ds(i * 16, 16))).astype(BF)

    def pair_add(b, u):
        pair_copy(b, u, mine(b, u)).wait_recv()
        slab = pair.at[b, unit_of[u]]
        accumulate(chunk(b, u, c), CH, lambda r: slab[r, :].astype(F32))

    def rs(b, rows, dst, idx, dest):
        return remote(sg.at[rows], dst, rs_send.at[b, idx], rs_recv.at[b, idx], (g, dest))

    def rs_start(b, rows, dst, idx, dest):
        start(rs(b, rows, dst, idx, dest))

    def rs_wait(b, dst, idx, size=CH):
        rs(b, mine(b, OWN, 0, size), dst, idx, to_y).wait_recv()

    def tile_copies(slot, j):
        cols = pl.ds(pl.multiple_of(j * 256, 256), 256)
        return (
            pltpu.make_async_copy(tile_in.at[slot], dwin_hbm.at[0, cols, :], t_sem.at[0, slot]),
            pltpu.make_async_copy(tile_out.at[slot], dwout_hbm.at[0, :, cols], t_sem.at[1, slot]),
        )

    def weight_tiles(first, last):
        @pl.loop(first, last)
        def _(j):
            slot = lax.rem(j, 2)
            cols = pl.ds(pl.multiple_of(j * 256, 256), 256)
            into, outof = tile_copies(slot, j)

            @pl.when(j >= 2)
            def _():
                into.wait()
                outof.wait()

            tile_in[slot] = jnp.dot(hg_t[...], xbuf[:, cols], preferred_element_type=F32).T
            into.start()
            tile_out[slot] = jnp.dot(act_t[...], gbuf[:, cols], preferred_element_type=F32)
            outof.start()

    def own_out(b):
        for a in range(2):
            if b == 0:
                own_copies[a].wait()
            a_wait(a, b)
            start(ag(a, b, mine(b, OWN), to_up, PIECE_M))
            start(ag(a, b, mine(b, OWN), to_down, PIECE_P))
            start(ag(a, b, mine(b, OWN), to_y, PIECE_Y))
            core_start(a, b, OWN)

    def near(a, b):
        ag_wait(a, b, mine(b, ZM), PIECE_M)
        start(ag(a, b, mine(b, ZM, 0, HALF), to_up, PIECE_A))
        core_start(a, b, ZM)
        ag_wait(a, b, mine(b, ZP), PIECE_P)
        start(ag(a, b, mine(b, ZP, HALF, HALF), to_down, PIECE_B))
        core_start(a, b, ZP)

    def side_wait(a, b):
        ag_wait(a, b, mine(b, YY), PIECE_Y)
        core_start(a, b, YY)

    def side_out(a, b):
        start(ag(a, b, mine(b, YY), to_up, PIECE_MY))
        start(ag(a, b, mine(b, YY), to_down, PIECE_PY))

    def far_out(a, b):
        ag_wait(a, b, mine(b, OO, 0, HALF), PIECE_A)
        ag_wait(a, b, mine(b, OO, HALF, HALF), PIECE_B)
        start(ag(a, b, mine(b, OO), to_y, PIECE_OY))
        core_start(a, b, OO)

    def land(a, b, u, piece):
        ag_wait(a, b, mine(b, u), piece)
        core_start(a, b, u)

    def leaves(b):
        pair_add(b, MY)
        rs_start(b, mine(b, MY), rs_leaf.at[b, 1], RS_LP, to_down)
        pair_add(b, PY)
        rs_start(b, mine(b, PY), rs_leaf.at[b, 0], RS_LM, to_up)

    def y_leaf(b):
        pair_add(b, OY)
        rs_start(b, mine(b, OY), rs_y1.at[b], RS_Y1, to_y)

    def far_sum(b):
        pair_add(b, OO)
        rs_wait(b, rs_y1.at[b], RS_Y1)
        accumulate(chunk(b, OO, c), CH, lambda r: rs_y1[b, r, :].astype(F32))
        rs_start(b, mine(b, OO, 0, HALF), rs_half.at[b, 0], RS_A, to_down)
        rs_start(b, mine(b, OO, HALF, HALF), rs_half.at[b, 1], RS_B, to_up)

    def near_free(b):
        rs_start(b, mine(b, ZM, HALF, HALF), rs_last.at[b, 1, pl.ds(HALF, HALF)], RS_P1, to_down)
        rs_start(b, mine(b, ZP, 0, HALF), rs_last.at[b, 0, pl.ds(0, HALF)], RS_M0, to_up)

    def near_sum(b):
        rs_wait(b, rs_half.at[b, 0], RS_A, HALF)
        accumulate(chunk(b, ZM, c), HALF, lambda r: rs_half[b, 0, r, :].astype(F32))
        rs_start(b, mine(b, ZM, 0, HALF), rs_last.at[b, 1, pl.ds(0, HALF)], RS_P0, to_down)
        rs_wait(b, rs_half.at[b, 1], RS_B, HALF)
        accumulate(chunk(b, ZP, c) + HALF, HALF, lambda r: rs_half[b, 1, r, :].astype(F32))
        rs_start(b, mine(b, ZP, HALF, HALF), rs_last.at[b, 0, pl.ds(HALF, HALF)], RS_M1, to_up)

    def side_sum(b):
        rs_wait(b, rs_leaf.at[b, 0], RS_LM)
        rs_wait(b, rs_leaf.at[b, 1], RS_LP)
        accumulate(
            chunk(b, YY, c),
            CH,
            lambda r: rs_leaf[b, 0, r, :].astype(F32) + rs_leaf[b, 1, r, :].astype(F32),
        )
        rs_start(b, mine(b, YY), rs_last.at[b, 2], RS_Y, to_y)

    def d_copy(i):
        b, k = hops[i]
        dest = partner(b, k)
        return remote(
            fin.at[ds(b * CH + lax.rem(x + k, 4) * SL, SL)],
            back.at[ds(g * SL, SL)],
            d_send.at[i],
            d_recv.at[i],
            dest,
        )

    def finish(b):
        rs_wait(b, rs_last.at[b, 0, pl.ds(0, HALF)], RS_M0, HALF)
        rs_wait(b, rs_last.at[b, 0, pl.ds(HALF, HALF)], RS_M1, HALF)
        rs_wait(b, rs_last.at[b, 1, pl.ds(0, HALF)], RS_P0, HALF)
        rs_wait(b, rs_last.at[b, 1, pl.ds(HALF, HALF)], RS_P1, HALF)
        rs_wait(b, rs_last.at[b, 2], RS_Y)

        @pl.loop(0, CH // 16)
        def _(i):
            rows = ds(chunk(b, OWN, c) + i * 16, 16)
            r = ds(i * 16, 16)
            total = sg[rows, :].astype(F32) + rs_last[b, 0, r, :].astype(F32)
            total = total + rs_last[b, 1, r, :].astype(F32) + rs_last[b, 2, r, :].astype(F32)
            fin[ds(b * CH + i * 16, 16), :] = total.astype(BF)

        for i in range(len(hops)):
            if hops[i][0] == b:
                start(d_copy(i))

    own_out(0)
    for w in w_copies:
        w.wait()
    near(0, 0)
    side_wait(0, 0)
    forward(0, (ZM, ZP))
    near(1, 0)
    side_out(0, 0)
    side_wait(1, 0)
    side_out(1, 0)
    forward(0, (OWN, YY))
    backward(0, (ZM, ZP))
    far_out(0, 0)
    backward(0, (OWN, YY))
    far_out(1, 0)
    own_out(1)
    for u in (ZM, ZP, OWN, YY):
        pair_add(0, u)
    land(0, 0, OY, PIECE_OY)
    forward(0, (OO, OY))
    land(0, 0, MY, PIECE_MY)
    land(0, 0, PY, PIECE_PY)
    forward(0, (MY, PY))
    land(1, 0, OY, PIECE_OY)
    backward(0, (OO, OY))
    land(1, 0, MY, PIECE_MY)
    land(1, 0, PY, PIECE_PY)
    y_leaf(0)
    backward(0, (MY, PY))
    leaves(0)

    near(0, 1)
    side_wait(0, 1)
    forward(1, (ZM, ZP))
    near(1, 1)
    side_out(0, 1)
    side_wait(1, 1)
    side_out(1, 1)
    far_sum(0)
    near_free(0)
    forward(1, (OWN, YY))
    backward(1, (ZM, ZP))
    far_out(0, 1)
    backward(1, (OWN, YY))
    far_out(1, 1)
    side_sum(0)
    for u in (ZM, ZP, OWN, YY):
        pair_add(1, u)
    land(0, 1, OY, PIECE_OY)
    forward(1, (OO, OY))
    land(0, 1, MY, PIECE_MY)
    land(0, 1, PY, PIECE_PY)
    forward(1, (MY, PY))
    land(1, 1, OY, PIECE_OY)
    backward(1, (OO, OY))
    y_leaf(1)
    land(1, 1, MY, PIECE_MY)
    land(1, 1, PY, PIECE_PY)
    backward(1, (MY, PY))
    leaves(1)
    near_sum(0)
    near_free(1)
    weight_tiles(0, 2)
    far_sum(1)
    finish(0)
    weight_tiles(2, 4)
    side_sum(1)
    near_sum(1)
    weight_tiles(4, 8)
    finish(1)
    own_rows = ds(g * SL, SL)
    back[own_rows, :] = fin[ds(x * SL, SL), :]
    for slot in range(2):
        into, outof = tile_copies(slot, 6 + slot)
        into.wait()
        outof.wait()
    for i, (b, k) in enumerate(hops):
        sender = (h if b == 0 else 1 - h) * 4 + source_x(k)
        remote(
            fin.at[pl.ds(0, SL)], back.at[ds(sender * SL, SL)], d_send.at[i], d_recv.at[i], (g, to_y)
        ).wait_recv()
    ret_ref[...] = back[...]
    for copy in pending:
        copy.wait_send()


def layer(chosen, counts, gates, tokens_in, out_grad, w_in, w_out):
    width = tokens_in.shape[1]
    hidden = w_in.shape[2]
    rows = chosen.shape[1] * chosen.shape[2]
    total = rows * lax.axis_size("fsdp")
    vmem, dma = pltpu.VMEM, pltpu.SemaphoreType.DMA
    in_vmem, in_hbm = pl.BlockSpec(memory_space=pltpu.VMEM), pl.BlockSpec(memory_space=pl.ANY)
    return pl.pallas_call(
        layer_kernel,
        out_shape=[
            jax.ShapeDtypeStruct((rows, width), BF),
            jax.ShapeDtypeStruct((1, width, hidden), F32),
            jax.ShapeDtypeStruct((1, hidden, width), F32),
        ],
        in_specs=[in_vmem] * 3 + [in_hbm] * 4,
        out_specs=[in_vmem, in_hbm, in_hbm],
        scratch_shapes=[
            vmem((rows, width), BF),
            vmem((rows, width), BF),
            vmem((rows, tokens_in.shape[0]), BF),
            vmem((total, width), BF),
            vmem((total, width), BF),
            vmem((width, hidden), BF),
            vmem((hidden, width), BF),
            vmem((hidden, total), BF),
            vmem((hidden, total), BF),
            vmem((total, hidden), F32),
            vmem((total, width), BF),
            vmem((2, 8, CH, width), BF),
            vmem((2, CH, width), BF),
            vmem((2, 2, HALF, width), BF),
            vmem((2, 2, CH, width), BF),
            vmem((2, 3, CH, width), BF),
            vmem((rows, width), BF),
            vmem((rows, width), BF),
            vmem((2, 256, hidden), F32),
            vmem((2, hidden, 256), F32),
            dma((2, 4)),
            dma((2, 7)),
            dma((2, 7)),
            dma((2,)),
            dma((2,)),
            dma((2, 2, 8)),
            dma((2, 2, 8)),
            dma((2, 2, 8)),
            dma((2, 2, 8)),
            dma((2, 8)),
            dma((2, 8)),
            dma((2, 10)),
            dma((2, 10)),
            dma((7,)),
            dma((7,)),
            dma((2, 2)),
        ],
        compiler_params=pltpu.CompilerParams(
            collective_id=0, has_side_effects=True, vmem_limit_bytes=62 * 1024 * 1024
        ),
        name="layer",
    )(chosen, counts, gates, tokens_in, out_grad, w_in, w_out)


def shards(tokens_in, out_grad, w_in, w_out, chosen, counts, gates):
    ret, grad_w_in, grad_w_out = layer(chosen, counts, gates, tokens_in, out_grad, w_in, w_out)
    grad_in = spread_rows(chosen, ret, tokens_in.shape[0])
    return (grad_in, grad_w_in, grad_w_out)


def solution(mesh):
    placed = (
        P(("group", "fsdp"), None),
        P(("group", "fsdp"), None),
        P("group", None, "fsdp"),
        P("group", "fsdp", None),
        P(("group", "fsdp"), None, None),
        P(("group", "fsdp"), None),
        P(("group", "fsdp"), None, None),
    )
    return jax.shard_map(
        shards,
        mesh=mesh,
        in_specs=placed,
        out_specs=(P(("group", "fsdp"), None), P("group", None, "fsdp"), P("group", "fsdp", None)),
        check_vma=False,
    )
```

```python
import jax
import jax.numpy as jnp
from jax import lax
from jax.experimental import pallas as pl
from jax.experimental.pallas import tpu as pltpu
from jax.sharding import PartitionSpec as P

MESH = pl.DeviceIdType.MESH
gelu_coef = 0.7978845608028654
BF = jnp.bfloat16
F32 = jnp.float32


def gelu_parts(hidden):
    inner_arg = gelu_coef * (hidden + 0.044715 * hidden * hidden * hidden)
    tangent = jnp.tanh(inner_arg)
    activation = 0.5 * hidden * (1.0 + tangent)
    slope = 0.5 * (1.0 + tangent) + 0.5 * hidden * (1.0 - tangent * tangent) * gelu_coef * (
        1.0 + 3.0 * 0.044715 * hidden * hidden
    )
    return (activation, slope)


def slot_column(table):
    experts, slots = table.shape
    spread = jnp.concatenate(
        [jnp.broadcast_to(table[e : e + 1, :], (slots, slots)) for e in range(experts)], axis=0
    )
    row = lax.broadcasted_iota(jnp.int32, spread.shape, 0)
    lane = lax.broadcasted_iota(jnp.int32, spread.shape, 1)
    picked = jnp.where(lax.rem(row, slots) == lane, spread, jnp.zeros_like(spread))
    return jnp.sum(picked, axis=1, keepdims=True)


def one_hot_rows(chosen, length):
    column = slot_column(chosen.astype(F32)).astype(jnp.int32)
    lanes = lax.broadcasted_iota(jnp.int32, (column.shape[0], length), 1)
    return jnp.where(lanes == column, jnp.float32(1.0), jnp.float32(0.0)).astype(BF)


def spread_kernel(chosen_ref, ret_ref, dwin_ref, dwout_ref, out_hbm, win_hbm, wout_hbm, tiles, sem):
    copies = [
        pltpu.make_async_copy(dwin_ref, win_hbm.at[0], sem.at[0]),
        pltpu.make_async_copy(dwout_ref, wout_hbm.at[0], sem.at[1]),
    ]
    for copy in copies:
        copy.start()
    count, size = tiles.shape[0], tiles.shape[1]
    column = slot_column(chosen_ref[0].astype(F32)).astype(jnp.int32)
    lanes = lax.broadcasted_iota(jnp.int32, (column.shape[0], size), 1)
    for i in range(count):
        hot = jnp.where(lanes + i * size == column, jnp.float32(1.0), jnp.float32(0.0)).astype(BF)
        tiles[i] = lax.dot_general(
            hot, ret_ref[...], (((0,), (0,)), ((), ())), preferred_element_type=F32
        ).astype(BF)
        copy = pltpu.make_async_copy(tiles.at[i], out_hbm.at[pl.ds(i * size, size)], sem.at[2 + i])
        copy.start()
        copies.append(copy)
    for copy in copies:
        copy.wait()


def spread_rows(chosen, ret, dwin, dwout, length):
    rows, width = ret.shape
    count = 4
    in_vmem, in_hbm = pl.BlockSpec(memory_space=pltpu.VMEM), pl.BlockSpec(memory_space=pltpu.HBM)
    return pl.pallas_call(
        spread_kernel,
        in_specs=[in_vmem] * 4,
        out_specs=[in_hbm] * 3,
        out_shape=[
            jax.ShapeDtypeStruct((length, width), BF),
            jax.ShapeDtypeStruct((1,) + dwin.shape, F32),
            jax.ShapeDtypeStruct((1,) + dwout.shape, F32),
        ],
        scratch_shapes=[
            pltpu.VMEM((count, length // count, width), BF),
            pltpu.SemaphoreType.DMA((2 + count,)),
        ],
        compiler_params=pltpu.CompilerParams(vmem_limit_bytes=12 * 1024 * 1024),
        name="spread_rows",
    )(chosen, ret, dwin, dwout)


OWN, YY, ZM, ZP, OO, OY, MY, PY = range(8)
PIECE_M, PIECE_P, PIECE_Y, PIECE_A, PIECE_B, PIECE_OY, PIECE_MY, PIECE_PY, PIECE_QM, PIECE_QP = range(10)
RS_Y1, RS_A, RS_B, RS_LM, RS_LP, RS_M0, RS_M1, RS_P0, RS_P1, RS_Y, RS_QM, RS_QP = range(12)
CH = 64
LAYER_VMEM = 52 * 1024 * 1024
HALF = CH // 2
SL = 16
QS = 16
PLACE = {
    (0, 0): (0, 0),
    (0, 1): (0, 1),
    (1, 0): (0, 2),
    (1, 1): (0, 3),
    (0, 2): (1, 0),
    (0, 3): (1, 1),
    (1, 2): (1, 2),
    (1, 3): (1, 3),
}
HOPS = [hop for hop in PLACE if hop != (0, 0)]


def layer_kernel(
    chosen_ref,
    counts_ref,
    gates_ref,
    tok_hbm,
    cot_hbm,
    win_hbm,
    wout_hbm,
    ret_ref,
    dwin_ref,
    dwout_ref,
    px,
    pg,
    hot,
    xbuf,
    gbuf,
    win,
    wout,
    act_t,
    hg_t,
    slope_buf,
    sg,
    pair,
    rs_y1,
    rs_half,
    rs_leaf,
    rs_last,
    rs_q,
    fin,
    back,
    tok_sem,
    a_send,
    a_recv,
    own_sem,
    w_sem,
    ag_send,
    ag_recv,
    core_send,
    core_recv,
    pr_send,
    pr_recv,
    rs_send,
    rs_recv,
    d_send,
    d_recv,
):
    g = lax.axis_index("group")
    f = lax.axis_index("fsdp")
    h, x = g // 4, lax.rem(g, 4)
    z, l, c = f // 4, lax.rem(f // 2, 2), lax.rem(f, 2)
    up, down, far = lax.rem(z + 1, 4), lax.rem(z + 3, 4), lax.rem(z + 2, 4)
    unit_of = {
        OWN: z * 2 + l,
        YY: z * 2 + (1 - l),
        ZM: down * 2 + l,
        ZP: up * 2 + l,
        OO: far * 2 + l,
        OY: far * 2 + (1 - l),
        MY: down * 2 + (1 - l),
        PY: up * 2 + (1 - l),
    }
    to_up, to_down = up * 4 + l * 2 + c, down * 4 + l * 2 + c
    to_y = z * 4 + (1 - l) * 2 + c
    to_core = z * 4 + l * 2 + (1 - c)
    batch_rows = 16 * CH

    def partner(flip, k):
        if flip:
            return ((1 - h) * 4 + lax.rem(x + k, 4), to_y)
        return (h * 4 + lax.rem(x + k, 4), f)

    def ds(start, size):
        return pl.ds(pl.multiple_of(start, 16), size)

    def chunk(b, u, which):
        return b * batch_rows + (unit_of[u] * 2 + which) * CH

    def mine(b, u, start=0, size=CH):
        return ds(chunk(b, u, c) + start, size)

    def other(b, u):
        return ds(chunk(b, u, 1 - c), CH)

    def unit_rows(b, u):
        return pl.ds(pl.multiple_of(b * batch_rows + unit_of[u] * 2 * CH, 2 * CH), 2 * CH)

    length = tok_hbm.shape[0]
    width = tok_hbm.shape[1]
    token_copies = []
    for a, source in enumerate((tok_hbm, cot_hbm)):
        for j in range(4):
            cols = pl.ds(j * (width // 4), width // 4)
            copy = pltpu.make_async_copy(
                source.at[:, cols], sg.at[pl.ds(a * length, length), cols], tok_sem.at[a, j]
            )
            copy.start()
            token_copies.append(copy)
    w_copies = [
        pltpu.make_async_copy(win_hbm.at[0], win, w_sem.at[0]),
        pltpu.make_async_copy(wout_hbm.at[0], wout, w_sem.at[1]),
    ]
    for w in w_copies:
        w.start()
    barrier = pltpu.get_barrier_semaphore()
    for hop in HOPS:
        pl.semaphore_signal(barrier, inc=1, device_id=partner(*hop), device_id_type=MESH)
    for d in (to_up, to_down, to_y, to_core):
        pl.semaphore_signal(barrier, inc=1, device_id=(g, d), device_id_type=MESH)

    hot[...] = one_hot_rows(chosen_ref[0], length)
    slot_iota = lax.broadcasted_iota(jnp.int32, chosen_ref.shape[1:], 1)
    experts = chosen_ref.shape[1]
    lane = lax.broadcasted_iota(jnp.int32, (experts, experts), 1)
    row = lax.broadcasted_iota(jnp.int32, (experts, experts), 0)
    limit = jnp.sum(
        jnp.where(lane == row, jnp.broadcast_to(counts_ref[...].astype(F32), (experts, experts)), 0.0),
        axis=1,
        keepdims=True,
    )
    live = jnp.where(slot_iota.astype(F32) < limit, gates_ref[0], jnp.float32(0.0))
    gate = slot_column(live)

    bufs = (xbuf, gbuf)
    picked = (px, pg)
    pending = []

    def start(copy):
        copy.start()
        pending.append(copy)

    def remote(src, dst, send, recv, dest):
        return pltpu.make_async_remote_copy(
            src_ref=src, dst_ref=dst, send_sem=send, recv_sem=recv, device_id=dest, device_id_type=MESH
        )

    def a_start(a, batch):
        for i, hop in enumerate(HOPS):
            b, place = PLACE[hop]
            if b == batch:
                dest = partner(*hop)
                start(
                    remote(
                        picked[a].at[ds(dest[0] * SL, SL)],
                        bufs[a].at[ds(b * batch_rows + dest[1] * CH + place * SL, SL)],
                        a_send.at[a, i],
                        a_recv.at[a, i],
                        dest,
                    )
                )

    def a_wait(a, batch):
        for i, hop in enumerate(HOPS):
            b, place = PLACE[hop]
            if b == batch:
                here = bufs[a].at[ds(b * batch_rows + f * CH + place * SL, SL)]
                remote(here, here, a_send.at[a, i], a_recv.at[a, i], (g, to_y)).wait_recv()

    own_copies = []
    for a in range(2):
        for j in range(4):
            cols = pl.ds(j * (width // 4), width // 4)
            token_copies[a * 4 + j].wait()
            rows = jnp.dot(hot[...], sg[pl.ds(a * length, length), cols], preferred_element_type=F32)
            picked[a][:, cols] = (rows if a == 0 else gate * rows).astype(BF)
        if a == 0:
            pl.semaphore_wait(barrier, len(HOPS) + 4)
        a_start(a, 0)
        own = pltpu.make_async_copy(
            picked[a].at[ds(g * SL, SL)], bufs[a].at[ds(f * CH, SL)], own_sem.at[a]
        )
        own.start()
        own_copies.append(own)
    for a in range(2):
        a_start(a, 1)

    def ag(a, b, rows, dest, piece):
        return remote(
            bufs[a].at[rows], bufs[a].at[rows], ag_send.at[a, b, piece], ag_recv.at[a, b, piece], (g, dest)
        )

    def ag_wait(a, b, rows, piece):
        ag(a, b, rows, to_y, piece).wait_recv()

    def core(a, b, u, rows):
        return remote(
            bufs[a].at[rows], bufs[a].at[rows], core_send.at[a, b, u], core_recv.at[a, b, u], (g, to_core)
        )

    def core_start(a, b, u):
        start(core(a, b, u, mine(b, u)))

    def core_wait(a, b, u):
        core(a, b, u, other(b, u)).wait_recv()

    def rows_of(ref, b, us):
        return jnp.concatenate([ref[unit_rows(b, u), :] for u in us], axis=0)

    def forward(b, us):
        for u in us:
            core_wait(0, b, u)
        hidden = jnp.dot(rows_of(xbuf, b, us), win[...], preferred_element_type=F32)
        activation, slope = gelu_parts(hidden)
        turned = activation.T.astype(BF)
        for i, u in enumerate(us):
            part = slice(i * 2 * CH, (i + 1) * 2 * CH)
            act_t[:, unit_rows(b, u)] = turned[:, part]
            slope_buf[unit_rows(b, u), :] = slope[part, :]

    def pair_copy(b, u, rows):
        return remote(
            sg.at[rows], pair.at[b, unit_of[u]], pr_send.at[b, u], pr_recv.at[b, u], (g, to_core)
        )

    def backward(b, us):
        for u in us:
            core_wait(1, b, u)
        back_hidden = lax.dot_general(
            rows_of(gbuf, b, us), wout[...], (((1,), (1,)), ((), ())), preferred_element_type=F32
        )
        hidden_grad = back_hidden * rows_of(slope_buf, b, us)
        turned = hidden_grad.T.astype(BF)
        for i, u in enumerate(us):
            hg_t[:, unit_rows(b, u)] = turned[:, i * 2 * CH : (i + 1) * 2 * CH]
        hidden_grad = hidden_grad.astype(BF)

        @pl.loop(0, 4)
        def _(j):
            cols = pl.ds(pl.multiple_of(j * 512, 512), 512)
            part = lax.dot_general(
                hidden_grad, win[cols, :], (((1,), (1,)), ((), ())), preferred_element_type=F32
            ).astype(BF)
            for i, u in enumerate(us):
                sg[unit_rows(b, u), cols] = part[i * 2 * CH : (i + 1) * 2 * CH, :]

        for u in us:
            start(pair_copy(b, u, other(b, u)))

    def accumulate(base, size, load):
        @pl.loop(0, size // 16)
        def _(i):
            rows = ds(base + i * 16, 16)
            total = sg[rows, :].astype(F32)
            sg[rows, :] = (total + load(ds(i * 16, 16))).astype(BF)

    def pair_add(b, u):
        pair_copy(b, u, mine(b, u)).wait_recv()
        slab = pair.at[b, unit_of[u]]
        accumulate(chunk(b, u, c), CH, lambda r: slab[r, :].astype(F32))

    def rs(b, rows, dst, idx, dest):
        return remote(sg.at[rows], dst, rs_send.at[b, idx], rs_recv.at[b, idx], (g, dest))

    def rs_start(b, rows, dst, idx, dest):
        start(rs(b, rows, dst, idx, dest))

    def rs_wait(b, dst, idx, size=CH):
        rs(b, mine(b, OWN, 0, size), dst, idx, to_y).wait_recv()

    def weight_tiles(b, first, last):
        rows = pl.ds(b * batch_rows, batch_rows)

        @pl.loop(first, last)
        def _(j):
            cols = pl.ds(pl.multiple_of(j * 256, 256), 256)
            into = jnp.dot(hg_t[:, rows], xbuf[rows, cols], preferred_element_type=F32).T
            outof = jnp.dot(act_t[:, rows], gbuf[rows, cols], preferred_element_type=F32)
            if b == 0:
                dwin_ref[cols, :] = into
                dwout_ref[:, cols] = outof
            else:
                dwin_ref[cols, :] += into
                dwout_ref[:, cols] += outof

    def own_out(b):
        for a in range(2):
            if b == 0:
                own_copies[a].wait()
            a_wait(a, b)
            start(ag(a, b, mine(b, OWN), to_up, PIECE_M))
            start(ag(a, b, mine(b, OWN), to_down, PIECE_P))
            start(ag(a, b, mine(b, OWN), to_y, PIECE_Y))
            core_start(a, b, OWN)

    def near(a, b):
        ag_wait(a, b, mine(b, ZM), PIECE_M)
        start(ag(a, b, mine(b, ZM, 0, HALF), to_up, PIECE_A))
        core_start(a, b, ZM)
        ag_wait(a, b, mine(b, ZP), PIECE_P)
        start(ag(a, b, mine(b, ZP, HALF, HALF), to_down, PIECE_B))
        core_start(a, b, ZP)
        if a == 0:
            start(ag(a, b, mine(b, ZM, 0, QS), to_y, PIECE_QM))
            start(ag(a, b, mine(b, ZP, CH - QS, QS), to_y, PIECE_QP))

    def side_wait(a, b):
        ag_wait(a, b, mine(b, YY), PIECE_Y)
        core_start(a, b, YY)

    def side_out(a, b):
        q = QS if a == 0 else 0
        start(ag(a, b, mine(b, YY, q, CH - q), to_up, PIECE_MY))
        start(ag(a, b, mine(b, YY, 0, CH - q), to_down, PIECE_PY))

    def far_out(a, b):
        ag_wait(a, b, mine(b, OO, 0, HALF), PIECE_A)
        ag_wait(a, b, mine(b, OO, HALF, HALF), PIECE_B)
        start(ag(a, b, mine(b, OO), to_y, PIECE_OY))
        core_start(a, b, OO)

    def far_land(a, b):
        ag_wait(a, b, mine(b, OY), PIECE_OY)
        core_start(a, b, OY)

    def side_land(a, b):
        q = QS if a == 0 else 0
        if q:
            ag_wait(a, b, mine(b, MY, 0, q), PIECE_QM)
            ag_wait(a, b, mine(b, PY, CH - q, q), PIECE_QP)
        ag_wait(a, b, mine(b, MY, q, CH - q), PIECE_MY)
        core_start(a, b, MY)
        ag_wait(a, b, mine(b, PY, 0, CH - q), PIECE_PY)
        core_start(a, b, PY)

    def leaves(b):
        pair_add(b, MY)
        rs_start(b, mine(b, MY, QS, CH - QS), rs_leaf.at[b, 1, pl.ds(QS, CH - QS)], RS_LP, to_down)
        rs_start(b, mine(b, MY, 0, QS), rs_q.at[b, 0], RS_QM, to_y)
        pair_add(b, PY)
        rs_start(b, mine(b, PY, 0, CH - QS), rs_leaf.at[b, 0, pl.ds(0, CH - QS)], RS_LM, to_up)
        rs_start(b, mine(b, PY, CH - QS, QS), rs_q.at[b, 1], RS_QP, to_y)

    def y_leaf(b):
        pair_add(b, OY)
        rs_start(b, mine(b, OY), rs_y1.at[b], RS_Y1, to_y)

    def far_sum(b):
        pair_add(b, OO)
        rs_wait(b, rs_y1.at[b], RS_Y1)
        accumulate(chunk(b, OO, c), CH, lambda r: rs_y1[b, r, :].astype(F32))
        rs_start(b, mine(b, OO, 0, HALF), rs_half.at[b, 0], RS_A, to_down)
        rs_start(b, mine(b, OO, HALF, HALF), rs_half.at[b, 1], RS_B, to_up)

    def near_free(b):
        rs_start(b, mine(b, ZM, HALF, HALF), rs_last.at[b, 1, pl.ds(HALF, HALF)], RS_P1, to_down)
        rs_start(b, mine(b, ZP, 0, HALF), rs_last.at[b, 0, pl.ds(0, HALF)], RS_M0, to_up)

    def near_sum(b):
        rs_wait(b, rs_q.at[b, 0], RS_QM, QS)
        accumulate(chunk(b, ZM, c), QS, lambda r: rs_q[b, 0, r, :].astype(F32))
        rs_wait(b, rs_half.at[b, 0], RS_A, HALF)
        accumulate(chunk(b, ZM, c), HALF, lambda r: rs_half[b, 0, r, :].astype(F32))
        rs_start(b, mine(b, ZM, 0, HALF), rs_last.at[b, 1, pl.ds(0, HALF)], RS_P0, to_down)
        rs_wait(b, rs_q.at[b, 1], RS_QP, QS)
        accumulate(chunk(b, ZP, c) + CH - QS, QS, lambda r: rs_q[b, 1, r, :].astype(F32))
        rs_wait(b, rs_half.at[b, 1], RS_B, HALF)
        accumulate(chunk(b, ZP, c) + HALF, HALF, lambda r: rs_half[b, 1, r, :].astype(F32))
        rs_start(b, mine(b, ZP, HALF, HALF), rs_last.at[b, 0, pl.ds(HALF, HALF)], RS_M1, to_up)

    def side_sum(b):
        rs_wait(b, rs_leaf.at[b, 0, pl.ds(0, CH - QS)], RS_LM, CH - QS)
        rs_wait(b, rs_leaf.at[b, 1, pl.ds(QS, CH - QS)], RS_LP, CH - QS)
        base = chunk(b, YY, c)
        low, high = rs_leaf.at[b, 0], rs_leaf.at[b, 1]
        accumulate(base, QS, lambda r: low[r, :].astype(F32))
        accumulate(
            base + QS,
            CH - 2 * QS,
            lambda r: low.at[pl.ds(QS, CH - 2 * QS)][r, :].astype(F32)
            + high.at[pl.ds(QS, CH - 2 * QS)][r, :].astype(F32),
        )
        accumulate(base + CH - QS, QS, lambda r: high.at[pl.ds(CH - QS, QS)][r, :].astype(F32))
        rs_start(b, mine(b, YY), rs_last.at[b, 2], RS_Y, to_y)

    def d_copy(i):
        flip, k = HOPS[i]
        b, place = PLACE[HOPS[i]]
        return remote(
            fin.at[pl.ds(b * CH + place * SL, SL)],
            back.at[ds(g * SL, SL)],
            d_send.at[i],
            d_recv.at[i],
            partner(flip, 4 - k),
        )

    def finish(b):
        rs_wait(b, rs_last.at[b, 0, pl.ds(0, HALF)], RS_M0, HALF)
        rs_wait(b, rs_last.at[b, 0, pl.ds(HALF, HALF)], RS_M1, HALF)
        rs_wait(b, rs_last.at[b, 1, pl.ds(0, HALF)], RS_P0, HALF)
        rs_wait(b, rs_last.at[b, 1, pl.ds(HALF, HALF)], RS_P1, HALF)
        rs_wait(b, rs_last.at[b, 2], RS_Y)

        @pl.loop(0, CH // 16)
        def _(i):
            rows = ds(chunk(b, OWN, c) + i * 16, 16)
            r = ds(i * 16, 16)
            total = sg[rows, :].astype(F32) + rs_last[b, 0, r, :].astype(F32)
            total = total + rs_last[b, 1, r, :].astype(F32) + rs_last[b, 2, r, :].astype(F32)
            fin[ds(b * CH + i * 16, 16), :] = total.astype(BF)

        for i, hop in enumerate(HOPS):
            if PLACE[hop][0] == b:
                start(d_copy(i))

    own_out(0)
    for w in w_copies:
        w.wait()
    near(0, 0)
    side_wait(0, 0)
    forward(0, (ZM, ZP))
    near(1, 0)
    side_out(0, 0)
    side_wait(1, 0)
    side_out(1, 0)
    forward(0, (OWN, YY))
    far_out(0, 0)
    backward(0, (ZM, ZP))
    far_out(1, 0)
    own_out(1)
    backward(0, (OWN, YY))
    for u in (ZM, ZP, OWN, YY):
        pair_add(0, u)
    far_land(0, 0)
    forward(0, (OO, OY))
    side_land(0, 0)
    forward(0, (MY, PY))
    far_land(1, 0)
    backward(0, (OO, OY))
    side_land(1, 0)
    y_leaf(0)
    backward(0, (MY, PY))
    leaves(0)

    near(0, 1)
    side_wait(0, 1)
    forward(1, (ZM, ZP))
    weight_tiles(0, 0, 3)
    near(1, 1)
    side_out(0, 1)
    side_wait(1, 1)
    side_out(1, 1)
    forward(1, (OWN, YY))
    backward(1, (ZM, ZP))
    far_sum(0)
    near_free(0)
    weight_tiles(0, 3, 4)
    far_out(0, 1)
    backward(1, (OWN, YY))
    far_out(1, 1)
    side_sum(0)
    for u in (ZM, ZP, OWN, YY):
        pair_add(1, u)
    weight_tiles(0, 4, 7)
    far_land(0, 1)
    forward(1, (OO, OY))
    side_land(0, 1)
    forward(1, (MY, PY))
    weight_tiles(0, 7, 8)
    far_land(1, 1)
    backward(1, (OO, OY))
    y_leaf(1)
    side_land(1, 1)
    backward(1, (MY, PY))
    leaves(1)
    near_sum(0)
    weight_tiles(1, 0, 4)
    far_sum(1)
    near_free(1)
    side_sum(1)
    weight_tiles(1, 4, 6)
    finish(0)
    near_sum(1)
    weight_tiles(1, 6, 8)
    finish(1)
    own_rows = ds(g * SL, SL)
    back[own_rows, :] = fin[pl.ds(0, SL), :]
    for i, hop in enumerate(HOPS):
        remote(
            fin.at[pl.ds(0, SL)], back.at[ds(partner(*hop)[0] * SL, SL)], d_send.at[i], d_recv.at[i], (g, to_y)
        ).wait_recv()
    ret_ref[...] = back[...]
    for copy in pending:
        copy.wait_send()


def layer(chosen, counts, gates, tokens_in, out_grad, w_in, w_out):
    width = tokens_in.shape[1]
    hidden = w_in.shape[2]
    rows = chosen.shape[1] * chosen.shape[2]
    total = rows * lax.axis_size("fsdp")
    vmem, dma = pltpu.VMEM, pltpu.SemaphoreType.DMA
    in_vmem, in_hbm = pl.BlockSpec(memory_space=pltpu.VMEM), pl.BlockSpec(memory_space=pltpu.HBM)
    return pl.pallas_call(
        layer_kernel,
        out_shape=[
            vmem((rows, width), BF),
            vmem((width, hidden), F32),
            vmem((hidden, width), F32),
        ],
        in_specs=[in_vmem] * 3 + [in_hbm] * 4,
        out_specs=[in_vmem] * 3,
        scratch_shapes=[
            vmem((rows, width), BF),
            vmem((rows, width), BF),
            vmem((rows, tokens_in.shape[0]), BF),
            vmem((total, width), BF),
            vmem((total, width), BF),
            vmem((width, hidden), BF),
            vmem((hidden, width), BF),
            vmem((hidden, total), BF),
            vmem((hidden, total), BF),
            vmem((total, hidden), F32),
            vmem((total, width), BF),
            vmem((2, 8, CH, width), BF),
            vmem((2, CH, width), BF),
            vmem((2, 2, HALF, width), BF),
            vmem((2, 2, CH, width), BF),
            vmem((2, 3, CH, width), BF),
            vmem((2, 2, QS, width), BF),
            vmem((rows, width), BF),
            vmem((rows, width), BF),
            dma((2, 4)),
            dma((2, 7)),
            dma((2, 7)),
            dma((2,)),
            dma((2,)),
            dma((2, 2, 10)),
            dma((2, 2, 10)),
            dma((2, 2, 8)),
            dma((2, 2, 8)),
            dma((2, 8)),
            dma((2, 8)),
            dma((2, 12)),
            dma((2, 12)),
            dma((7,)),
            dma((7,)),
        ],
        compiler_params=pltpu.CompilerParams(
            collective_id=0, has_side_effects=True, vmem_limit_bytes=LAYER_VMEM
        ),
        name="layer",
    )(chosen, counts, gates, tokens_in, out_grad, w_in, w_out)


def shards(tokens_in, out_grad, w_in, w_out, chosen, counts, gates):
    ret, dwin, dwout = layer(chosen, counts, gates, tokens_in, out_grad, w_in, w_out)
    return spread_rows(chosen, ret, dwin, dwout, tokens_in.shape[0])


def solution(mesh):
    placed = (
        P(("group", "fsdp"), None),
        P(("group", "fsdp"), None),
        P("group", None, "fsdp"),
        P("group", "fsdp", None),
        P(("group", "fsdp"), None, None),
        P(("group", "fsdp"), None),
        P(("group", "fsdp"), None, None),
    )
    return jax.shard_map(
        shards,
        mesh=mesh,
        in_specs=placed,
        out_specs=(P(("group", "fsdp"), None), P("group", None, "fsdp"), P("group", "fsdp", None)),
        check_vma=False,
    )
```

```python
import jax
import jax.numpy as jnp
from jax import lax
from jax.experimental import pallas as pl
from jax.experimental.pallas import tpu as pltpu
from jax.sharding import PartitionSpec as P

MESH = pl.DeviceIdType.MESH
gelu_coef = 0.7978845608028654
BF = jnp.bfloat16
F32 = jnp.float32


def gelu_parts(hidden):
    inner_arg = gelu_coef * (hidden + 0.044715 * hidden * hidden * hidden)
    tangent = jnp.tanh(inner_arg)
    activation = 0.5 * hidden * (1.0 + tangent)
    slope = 0.5 * (1.0 + tangent) + 0.5 * hidden * (1.0 - tangent * tangent) * gelu_coef * (
        1.0 + 3.0 * 0.044715 * hidden * hidden
    )
    return (activation, slope)


def slot_column(table):
    experts, slots = table.shape
    spread = jnp.concatenate(
        [jnp.broadcast_to(table[e : e + 1, :], (slots, slots)) for e in range(experts)], axis=0
    )
    row = lax.broadcasted_iota(jnp.int32, spread.shape, 0)
    lane = lax.broadcasted_iota(jnp.int32, spread.shape, 1)
    picked = jnp.where(lax.rem(row, slots) == lane, spread, jnp.zeros_like(spread))
    return jnp.sum(picked, axis=1, keepdims=True)


def one_hot_rows(chosen, length):
    column = slot_column(chosen.astype(F32)).astype(jnp.int32)
    lanes = lax.broadcasted_iota(jnp.int32, (column.shape[0], length), 1)
    return jnp.where(lanes == column, jnp.float32(1.0), jnp.float32(0.0)).astype(BF)


def spread_kernel(chosen_ref, ret_ref, dwin_ref, dwout_ref, out_hbm, win_hbm, wout_hbm, tiles, sem):
    copies = [
        pltpu.make_async_copy(dwin_ref, win_hbm.at[0], sem.at[0]),
        pltpu.make_async_copy(dwout_ref, wout_hbm.at[0], sem.at[1]),
    ]
    for copy in copies:
        copy.start()
    count, size = tiles.shape[0], tiles.shape[1]
    column = slot_column(chosen_ref[0].astype(F32)).astype(jnp.int32)
    lanes = lax.broadcasted_iota(jnp.int32, (column.shape[0], size), 1)
    for i in range(count):
        hot = jnp.where(lanes + i * size == column, jnp.float32(1.0), jnp.float32(0.0)).astype(BF)
        tiles[i] = lax.dot_general(
            hot, ret_ref[...], (((0,), (0,)), ((), ())), preferred_element_type=F32
        ).astype(BF)
        copy = pltpu.make_async_copy(tiles.at[i], out_hbm.at[pl.ds(i * size, size)], sem.at[2 + i])
        copy.start()
        copies.append(copy)
    for copy in copies:
        copy.wait()


def spread_rows(chosen, ret, dwin, dwout, length):
    rows, width = ret.shape
    count = 4
    in_vmem, in_hbm = pl.BlockSpec(memory_space=pltpu.VMEM), pl.BlockSpec(memory_space=pltpu.HBM)
    return pl.pallas_call(
        spread_kernel,
        in_specs=[in_vmem] * 4,
        out_specs=[in_hbm] * 3,
        out_shape=[
            jax.ShapeDtypeStruct((length, width), BF),
            jax.ShapeDtypeStruct((1,) + dwin.shape, F32),
            jax.ShapeDtypeStruct((1,) + dwout.shape, F32),
        ],
        scratch_shapes=[
            pltpu.VMEM((count, length // count, width), BF),
            pltpu.SemaphoreType.DMA((2 + count,)),
        ],
        compiler_params=pltpu.CompilerParams(vmem_limit_bytes=12 * 1024 * 1024),
        name="spread_rows",
    )(chosen, ret, dwin, dwout)


OWN, YY, ZM, ZP, OO, OY, MY, PY = range(8)
PIECE_M, PIECE_P, PIECE_Y, PIECE_A, PIECE_B, PIECE_OY, PIECE_MY, PIECE_PY, PIECE_QM, PIECE_QP = range(10)
RS_Y1, RS_A, RS_B, RS_LM, RS_LP, RS_M0, RS_M1, RS_P0, RS_P1, RS_Y, RS_QM, RS_QP = range(12)
CH = 64
LAYER_VMEM = 52 * 1024 * 1024
HALF = CH // 2
SL = 16
QS = 16
PLACE = {
    (0, 0): (0, 0),
    (0, 1): (0, 1),
    (1, 0): (0, 2),
    (1, 1): (0, 3),
    (0, 2): (1, 0),
    (0, 3): (1, 1),
    (1, 2): (1, 2),
    (1, 3): (1, 3),
}
HOPS = [hop for hop in PLACE if hop != (0, 0)]


def layer_kernel(
    chosen_ref,
    counts_ref,
    gates_ref,
    tok_hbm,
    cot_hbm,
    win_hbm,
    wout_hbm,
    ret_ref,
    dwin_ref,
    dwout_ref,
    px,
    pg,
    hot,
    xbuf,
    gbuf,
    win,
    wout,
    act_t,
    hg_t,
    slope_buf,
    sg,
    pair,
    rs_y1,
    rs_half,
    rs_leaf,
    rs_last,
    rs_q,
    fin,
    back,
    tok_sem,
    a_send,
    a_recv,
    own_sem,
    w_sem,
    ag_send,
    ag_recv,
    core_send,
    core_recv,
    pr_send,
    pr_recv,
    rs_send,
    rs_recv,
    d_send,
    d_recv,
):
    g = lax.axis_index("group")
    f = lax.axis_index("fsdp")
    h, x = g // 4, lax.rem(g, 4)
    z, l, c = f // 4, lax.rem(f // 2, 2), lax.rem(f, 2)
    up, down, far = lax.rem(z + 1, 4), lax.rem(z + 3, 4), lax.rem(z + 2, 4)
    unit_of = {
        OWN: z * 2 + l,
        YY: z * 2 + (1 - l),
        ZM: down * 2 + l,
        ZP: up * 2 + l,
        OO: far * 2 + l,
        OY: far * 2 + (1 - l),
        MY: down * 2 + (1 - l),
        PY: up * 2 + (1 - l),
    }
    to_up, to_down = up * 4 + l * 2 + c, down * 4 + l * 2 + c
    to_y = z * 4 + (1 - l) * 2 + c
    to_core = z * 4 + l * 2 + (1 - c)
    batch_rows = 16 * CH

    def partner(flip, k):
        if flip:
            return ((1 - h) * 4 + lax.rem(x + k, 4), to_y)
        return (h * 4 + lax.rem(x + k, 4), f)

    def ds(start, size):
        return pl.ds(pl.multiple_of(start, 16), size)

    def chunk(b, u, which):
        return b * batch_rows + (unit_of[u] * 2 + which) * CH

    def mine(b, u, start=0, size=CH):
        return ds(chunk(b, u, c) + start, size)

    def other(b, u):
        return ds(chunk(b, u, 1 - c), CH)

    def unit_rows(b, u):
        return pl.ds(pl.multiple_of(b * batch_rows + unit_of[u] * 2 * CH, 2 * CH), 2 * CH)

    length = tok_hbm.shape[0]
    width = tok_hbm.shape[1]
    token_copies = []
    for a, source in enumerate((tok_hbm, cot_hbm)):
        for j in range(4):
            cols = pl.ds(j * (width // 4), width // 4)
            copy = pltpu.make_async_copy(
                source.at[:, cols], sg.at[pl.ds(a * length, length), cols], tok_sem.at[a, j]
            )
            copy.start()
            token_copies.append(copy)
    w_copies = [
        pltpu.make_async_copy(win_hbm.at[0], win, w_sem.at[0]),
        pltpu.make_async_copy(wout_hbm.at[0], wout, w_sem.at[1]),
    ]
    barrier = pltpu.get_barrier_semaphore()
    for hop in HOPS:
        pl.semaphore_signal(barrier, inc=1, device_id=partner(*hop), device_id_type=MESH)
    for d in (to_up, to_down, to_y, to_core):
        pl.semaphore_signal(barrier, inc=1, device_id=(g, d), device_id_type=MESH)

    hot[...] = one_hot_rows(chosen_ref[0], length)
    slot_iota = lax.broadcasted_iota(jnp.int32, chosen_ref.shape[1:], 1)
    experts = chosen_ref.shape[1]
    lane = lax.broadcasted_iota(jnp.int32, (experts, experts), 1)
    row = lax.broadcasted_iota(jnp.int32, (experts, experts), 0)
    limit = jnp.sum(
        jnp.where(lane == row, jnp.broadcast_to(counts_ref[...].astype(F32), (experts, experts)), 0.0),
        axis=1,
        keepdims=True,
    )
    live = jnp.where(slot_iota.astype(F32) < limit, gates_ref[0], jnp.float32(0.0))
    gate = slot_column(live)

    bufs = (xbuf, gbuf)
    picked = (px, pg)
    pending = []

    def start(copy):
        copy.start()
        pending.append(copy)

    def remote(src, dst, send, recv, dest):
        return pltpu.make_async_remote_copy(
            src_ref=src, dst_ref=dst, send_sem=send, recv_sem=recv, device_id=dest, device_id_type=MESH
        )

    def a_start(a, batch):
        for i, hop in enumerate(HOPS):
            b, place = PLACE[hop]
            if b == batch:
                dest = partner(*hop)
                start(
                    remote(
                        picked[a].at[ds(dest[0] * SL, SL)],
                        bufs[a].at[ds(b * batch_rows + dest[1] * CH + place * SL, SL)],
                        a_send.at[a, i],
                        a_recv.at[a, i],
                        dest,
                    )
                )

    def a_wait(a, batch):
        for i, hop in enumerate(HOPS):
            b, place = PLACE[hop]
            if b == batch:
                here = bufs[a].at[ds(b * batch_rows + f * CH + place * SL, SL)]
                remote(here, here, a_send.at[a, i], a_recv.at[a, i], (g, to_y)).wait_recv()

    own_copies = []
    for a in range(2):
        for j in range(4):
            cols = pl.ds(j * (width // 4), width // 4)
            token_copies[a * 4 + j].wait()
            rows = jnp.dot(hot[...], sg[pl.ds(a * length, length), cols], preferred_element_type=F32)
            picked[a][:, cols] = (rows if a == 0 else gate * rows).astype(BF)
        if a == 0:
            pl.semaphore_wait(barrier, len(HOPS) + 4)
        a_start(a, 0)
        own = pltpu.make_async_copy(
            picked[a].at[ds(g * SL, SL)], bufs[a].at[ds(f * CH, SL)], own_sem.at[a]
        )
        own.start()
        own_copies.append(own)
    for a in range(2):
        a_start(a, 1)
    for w in w_copies:
        w.start()

    def ag(a, b, rows, dest, piece):
        return remote(
            bufs[a].at[rows], bufs[a].at[rows], ag_send.at[a, b, piece], ag_recv.at[a, b, piece], (g, dest)
        )

    def ag_wait(a, b, rows, piece):
        ag(a, b, rows, to_y, piece).wait_recv()

    def core(a, b, u, rows):
        return remote(
            bufs[a].at[rows], bufs[a].at[rows], core_send.at[a, b, u], core_recv.at[a, b, u], (g, to_core)
        )

    def core_start(a, b, u):
        start(core(a, b, u, mine(b, u)))

    def core_wait(a, b, u):
        core(a, b, u, other(b, u)).wait_recv()

    def rows_of(ref, b, us):
        return jnp.concatenate([ref[unit_rows(b, u), :] for u in us], axis=0)

    def forward(b, us):
        for u in us:
            core_wait(0, b, u)
        hidden = jnp.dot(rows_of(xbuf, b, us), win[...], preferred_element_type=F32)
        activation, slope = gelu_parts(hidden)
        turned = activation.T.astype(BF)
        for i, u in enumerate(us):
            part = slice(i * 2 * CH, (i + 1) * 2 * CH)
            act_t[:, unit_rows(b, u)] = turned[:, part]
            slope_buf[unit_rows(b, u), :] = slope[part, :]

    def pair_copy(b, u, rows):
        return remote(
            sg.at[rows], pair.at[b, unit_of[u]], pr_send.at[b, u], pr_recv.at[b, u], (g, to_core)
        )

    def backward(b, us):
        for u in us:
            core_wait(1, b, u)
        back_hidden = lax.dot_general(
            rows_of(gbuf, b, us), wout[...], (((1,), (1,)), ((), ())), preferred_element_type=F32
        )
        hidden_grad = back_hidden * rows_of(slope_buf, b, us)
        turned = hidden_grad.T.astype(BF)
        for i, u in enumerate(us):
            hg_t[:, unit_rows(b, u)] = turned[:, i * 2 * CH : (i + 1) * 2 * CH]
        hidden_grad = hidden_grad.astype(BF)

        @pl.loop(0, 4)
        def _(j):
            cols = pl.ds(pl.multiple_of(j * 512, 512), 512)
            part = lax.dot_general(
                hidden_grad, win[cols, :], (((1,), (1,)), ((), ())), preferred_element_type=F32
            ).astype(BF)
            for i, u in enumerate(us):
                sg[unit_rows(b, u), cols] = part[i * 2 * CH : (i + 1) * 2 * CH, :]

        for u in us:
            start(pair_copy(b, u, other(b, u)))

    def accumulate(base, size, load):
        @pl.loop(0, size // 16)
        def _(i):
            rows = ds(base + i * 16, 16)
            total = sg[rows, :].astype(F32)
            sg[rows, :] = (total + load(ds(i * 16, 16))).astype(BF)

    def pair_add(b, u):
        pair_copy(b, u, mine(b, u)).wait_recv()
        slab = pair.at[b, unit_of[u]]
        accumulate(chunk(b, u, c), CH, lambda r: slab[r, :].astype(F32))

    def rs(b, rows, dst, idx, dest):
        return remote(sg.at[rows], dst, rs_send.at[b, idx], rs_recv.at[b, idx], (g, dest))

    def rs_start(b, rows, dst, idx, dest):
        start(rs(b, rows, dst, idx, dest))

    def rs_wait(b, dst, idx, size=CH):
        rs(b, mine(b, OWN, 0, size), dst, idx, to_y).wait_recv()

    def weight_tiles(b, first, last):
        rows = pl.ds(b * batch_rows, batch_rows)

        @pl.loop(first, last)
        def _(j):
            cols = pl.ds(pl.multiple_of(j * 256, 256), 256)
            into = jnp.dot(hg_t[:, rows], xbuf[rows, cols], preferred_element_type=F32).T
            outof = jnp.dot(act_t[:, rows], gbuf[rows, cols], preferred_element_type=F32)
            if b == 0:
                dwin_ref[cols, :] = into
                dwout_ref[:, cols] = outof
            else:
                dwin_ref[cols, :] += into
                dwout_ref[:, cols] += outof

    def own_out(b):
        for a in range(2):
            if b == 0:
                own_copies[a].wait()
            a_wait(a, b)
            start(ag(a, b, mine(b, OWN), to_up, PIECE_M))
            start(ag(a, b, mine(b, OWN), to_down, PIECE_P))
            start(ag(a, b, mine(b, OWN), to_y, PIECE_Y))
            core_start(a, b, OWN)

    def near(a, b):
        ag_wait(a, b, mine(b, ZM), PIECE_M)
        start(ag(a, b, mine(b, ZM, 0, HALF), to_up, PIECE_A))
        core_start(a, b, ZM)
        ag_wait(a, b, mine(b, ZP), PIECE_P)
        start(ag(a, b, mine(b, ZP, HALF, HALF), to_down, PIECE_B))
        core_start(a, b, ZP)
        if a == 0:
            start(ag(a, b, mine(b, ZM, 0, QS), to_y, PIECE_QM))
            start(ag(a, b, mine(b, ZP, CH - QS, QS), to_y, PIECE_QP))

    def side_wait(a, b):
        ag_wait(a, b, mine(b, YY), PIECE_Y)
        core_start(a, b, YY)

    def side_out(a, b):
        q = QS if a == 0 else 0
        start(ag(a, b, mine(b, YY, q, CH - q), to_up, PIECE_MY))
        start(ag(a, b, mine(b, YY, 0, CH - q), to_down, PIECE_PY))

    def far_out(a, b):
        ag_wait(a, b, mine(b, OO, 0, HALF), PIECE_A)
        ag_wait(a, b, mine(b, OO, HALF, HALF), PIECE_B)
        start(ag(a, b, mine(b, OO), to_y, PIECE_OY))
        core_start(a, b, OO)

    def far_land(a, b):
        ag_wait(a, b, mine(b, OY), PIECE_OY)
        core_start(a, b, OY)

    def side_land(a, b):
        q = QS if a == 0 else 0
        if q:
            ag_wait(a, b, mine(b, MY, 0, q), PIECE_QM)
            ag_wait(a, b, mine(b, PY, CH - q, q), PIECE_QP)
        ag_wait(a, b, mine(b, MY, q, CH - q), PIECE_MY)
        core_start(a, b, MY)
        ag_wait(a, b, mine(b, PY, 0, CH - q), PIECE_PY)
        core_start(a, b, PY)

    def leaves(b):
        pair_add(b, MY)
        rs_start(b, mine(b, MY, QS, CH - QS), rs_leaf.at[b, 1, pl.ds(QS, CH - QS)], RS_LP, to_down)
        rs_start(b, mine(b, MY, 0, QS), rs_q.at[b, 0], RS_QM, to_y)
        pair_add(b, PY)
        rs_start(b, mine(b, PY, 0, CH - QS), rs_leaf.at[b, 0, pl.ds(0, CH - QS)], RS_LM, to_up)
        rs_start(b, mine(b, PY, CH - QS, QS), rs_q.at[b, 1], RS_QP, to_y)

    def y_leaf(b):
        pair_add(b, OY)
        rs_start(b, mine(b, OY), rs_y1.at[b], RS_Y1, to_y)

    def far_sum(b):
        pair_add(b, OO)
        rs_wait(b, rs_y1.at[b], RS_Y1)
        accumulate(chunk(b, OO, c), CH, lambda r: rs_y1[b, r, :].astype(F32))
        rs_start(b, mine(b, OO, 0, HALF), rs_half.at[b, 0], RS_A, to_down)
        rs_start(b, mine(b, OO, HALF, HALF), rs_half.at[b, 1], RS_B, to_up)

    def near_free(b):
        rs_start(b, mine(b, ZM, HALF, HALF), rs_last.at[b, 1, pl.ds(HALF, HALF)], RS_P1, to_down)
        rs_start(b, mine(b, ZP, 0, HALF), rs_last.at[b, 0, pl.ds(0, HALF)], RS_M0, to_up)

    def near_sum(b):
        rs_wait(b, rs_q.at[b, 0], RS_QM, QS)
        accumulate(chunk(b, ZM, c), QS, lambda r: rs_q[b, 0, r, :].astype(F32))
        rs_wait(b, rs_half.at[b, 0], RS_A, HALF)
        accumulate(chunk(b, ZM, c), HALF, lambda r: rs_half[b, 0, r, :].astype(F32))
        rs_start(b, mine(b, ZM, 0, HALF), rs_last.at[b, 1, pl.ds(0, HALF)], RS_P0, to_down)
        rs_wait(b, rs_q.at[b, 1], RS_QP, QS)
        accumulate(chunk(b, ZP, c) + CH - QS, QS, lambda r: rs_q[b, 1, r, :].astype(F32))
        rs_wait(b, rs_half.at[b, 1], RS_B, HALF)
        accumulate(chunk(b, ZP, c) + HALF, HALF, lambda r: rs_half[b, 1, r, :].astype(F32))
        rs_start(b, mine(b, ZP, HALF, HALF), rs_last.at[b, 0, pl.ds(HALF, HALF)], RS_M1, to_up)

    def side_sum(b):
        rs_wait(b, rs_leaf.at[b, 0, pl.ds(0, CH - QS)], RS_LM, CH - QS)
        rs_wait(b, rs_leaf.at[b, 1, pl.ds(QS, CH - QS)], RS_LP, CH - QS)
        base = chunk(b, YY, c)
        low, high = rs_leaf.at[b, 0], rs_leaf.at[b, 1]
        accumulate(base, QS, lambda r: low[r, :].astype(F32))
        accumulate(
            base + QS,
            CH - 2 * QS,
            lambda r: low.at[pl.ds(QS, CH - 2 * QS)][r, :].astype(F32)
            + high.at[pl.ds(QS, CH - 2 * QS)][r, :].astype(F32),
        )
        accumulate(base + CH - QS, QS, lambda r: high.at[pl.ds(CH - QS, QS)][r, :].astype(F32))
        rs_start(b, mine(b, YY), rs_last.at[b, 2], RS_Y, to_y)

    def d_copy(i):
        flip, k = HOPS[i]
        b, place = PLACE[HOPS[i]]
        return remote(
            fin.at[pl.ds(b * CH + place * SL, SL)],
            back.at[ds(g * SL, SL)],
            d_send.at[i],
            d_recv.at[i],
            partner(flip, 4 - k),
        )

    def finish(b):
        rs_wait(b, rs_last.at[b, 0, pl.ds(0, HALF)], RS_M0, HALF)
        rs_wait(b, rs_last.at[b, 0, pl.ds(HALF, HALF)], RS_M1, HALF)
        rs_wait(b, rs_last.at[b, 1, pl.ds(0, HALF)], RS_P0, HALF)
        rs_wait(b, rs_last.at[b, 1, pl.ds(HALF, HALF)], RS_P1, HALF)
        rs_wait(b, rs_last.at[b, 2], RS_Y)

        @pl.loop(0, CH // 16)
        def _(i):
            rows = ds(chunk(b, OWN, c) + i * 16, 16)
            r = ds(i * 16, 16)
            total = sg[rows, :].astype(F32) + rs_last[b, 0, r, :].astype(F32)
            total = total + rs_last[b, 1, r, :].astype(F32) + rs_last[b, 2, r, :].astype(F32)
            fin[ds(b * CH + i * 16, 16), :] = total.astype(BF)

        for i, hop in enumerate(HOPS):
            if PLACE[hop][0] == b:
                start(d_copy(i))

    own_out(0)
    for w in w_copies:
        w.wait()
    near(0, 0)
    side_wait(0, 0)
    forward(0, (ZM, ZP))
    near(1, 0)
    side_out(0, 0)
    side_wait(1, 0)
    side_out(1, 0)
    forward(0, (OWN, YY))
    far_out(0, 0)
    backward(0, (ZM, ZP))
    far_out(1, 0)
    own_out(1)
    backward(0, (OWN, YY))
    for u in (ZM, ZP, OWN, YY):
        pair_add(0, u)
    far_land(0, 0)
    forward(0, (OO, OY))
    side_land(0, 0)
    forward(0, (MY, PY))
    far_land(1, 0)
    backward(0, (OO, OY))
    side_land(1, 0)
    y_leaf(0)
    backward(0, (MY, PY))
    leaves(0)

    near(0, 1)
    side_wait(0, 1)
    forward(1, (ZM, ZP))
    weight_tiles(0, 0, 3)
    near(1, 1)
    side_out(0, 1)
    side_wait(1, 1)
    side_out(1, 1)
    forward(1, (OWN, YY))
    backward(1, (ZM, ZP))
    far_sum(0)
    near_free(0)
    weight_tiles(0, 3, 4)
    far_out(0, 1)
    backward(1, (OWN, YY))
    far_out(1, 1)
    side_sum(0)
    for u in (ZM, ZP, OWN, YY):
        pair_add(1, u)
    weight_tiles(0, 4, 7)
    far_land(0, 1)
    forward(1, (OO, OY))
    side_land(0, 1)
    forward(1, (MY, PY))
    weight_tiles(0, 7, 8)
    far_land(1, 1)
    backward(1, (OO, OY))
    side_land(1, 1)
    y_leaf(1)
    backward(1, (MY, PY))
    near_sum(0)
    leaves(1)
    weight_tiles(1, 0, 4)
    far_sum(1)
    near_free(1)
    weight_tiles(1, 4, 6)
    side_sum(1)
    finish(0)
    weight_tiles(1, 6, 8)
    near_sum(1)
    finish(1)
    own_rows = ds(g * SL, SL)
    back[own_rows, :] = fin[pl.ds(0, SL), :]
    for i, hop in enumerate(HOPS):
        remote(
            fin.at[pl.ds(0, SL)], back.at[ds(partner(*hop)[0] * SL, SL)], d_send.at[i], d_recv.at[i], (g, to_y)
        ).wait_recv()
    ret_ref[...] = back[...]
    for copy in pending:
        copy.wait_send()


def layer(chosen, counts, gates, tokens_in, out_grad, w_in, w_out):
    width = tokens_in.shape[1]
    hidden = w_in.shape[2]
    rows = chosen.shape[1] * chosen.shape[2]
    total = rows * lax.axis_size("fsdp")
    vmem, dma = pltpu.VMEM, pltpu.SemaphoreType.DMA
    in_vmem, in_hbm = pl.BlockSpec(memory_space=pltpu.VMEM), pl.BlockSpec(memory_space=pltpu.HBM)
    return pl.pallas_call(
        layer_kernel,
        out_shape=[
            vmem((rows, width), BF),
            vmem((width, hidden), F32),
            vmem((hidden, width), F32),
        ],
        in_specs=[in_vmem] * 3 + [in_hbm] * 4,
        out_specs=[in_vmem] * 3,
        scratch_shapes=[
            vmem((rows, width), BF),
            vmem((rows, width), BF),
            vmem((rows, tokens_in.shape[0]), BF),
            vmem((total, width), BF),
            vmem((total, width), BF),
            vmem((width, hidden), BF),
            vmem((hidden, width), BF),
            vmem((hidden, total), BF),
            vmem((hidden, total), BF),
            vmem((total, hidden), F32),
            vmem((total, width), BF),
            vmem((2, 8, CH, width), BF),
            vmem((2, CH, width), BF),
            vmem((2, 2, HALF, width), BF),
            vmem((2, 2, CH, width), BF),
            vmem((2, 3, CH, width), BF),
            vmem((2, 2, QS, width), BF),
            vmem((rows, width), BF),
            vmem((rows, width), BF),
            dma((2, 4)),
            dma((2, 7)),
            dma((2, 7)),
            dma((2,)),
            dma((2,)),
            dma((2, 2, 10)),
            dma((2, 2, 10)),
            dma((2, 2, 8)),
            dma((2, 2, 8)),
            dma((2, 8)),
            dma((2, 8)),
            dma((2, 12)),
            dma((2, 12)),
            dma((7,)),
            dma((7,)),
        ],
        compiler_params=pltpu.CompilerParams(
            collective_id=0, has_side_effects=True, vmem_limit_bytes=LAYER_VMEM
        ),
        name="layer",
    )(chosen, counts, gates, tokens_in, out_grad, w_in, w_out)


def shards(tokens_in, out_grad, w_in, w_out, chosen, counts, gates):
    ret, dwin, dwout = layer(chosen, counts, gates, tokens_in, out_grad, w_in, w_out)
    return spread_rows(chosen, ret, dwin, dwout, tokens_in.shape[0])


def solution(mesh):
    placed = (
        P(("group", "fsdp"), None),
        P(("group", "fsdp"), None),
        P("group", None, "fsdp"),
        P("group", "fsdp", None),
        P(("group", "fsdp"), None, None),
        P(("group", "fsdp"), None),
        P(("group", "fsdp"), None, None),
    )
    return jax.shard_map(
        shards,
        mesh=mesh,
        in_specs=placed,
        out_specs=(P(("group", "fsdp"), None), P("group", None, "fsdp"), P("group", "fsdp", None)),
        check_vma=False,
    )
```
